256 devices in a mesh: expert: 8 (over y, core), dp: 32 (over x, z).
Axes of the slice: x: 4, y: 4, z: 8, core: 2. Of those that a mesh axis runs over, the one named last changes fastest.
Arguments:
- hidden: bfloat16 [8, 14336, 1024], P('expert', 'dp'), may hold values from -6 to 6
- weight_codes: int32 [8, 14336, 2048], P('expert', 'dp'), may hold values from -8 to 7
- group_scales: float32 [8, 448, 2048], P('expert', 'dp'), may hold values from 0.0006681531 to 0.0050111483
- expert_index: int32 [4096, 2], P('expert'), may hold values from 0 to 7, all different within a row
- gate_values: float32 [4096, 2], P('expert'), may hold values from 0.2 to 1
- output_grad: bfloat16 [4096, 2048], P('expert', 'dp'), may hold values from -6 to 6
Outputs:
- combined: bfloat16 [4096, 2048], P('expert', 'dp')
- gate_grad: float32 [4096, 2], P('expert')
- hidden_grad: bfloat16 [8, 14336, 1024], P('expert', 'dp')
- weight_grad: float32 [8, 14336, 2048], P('expert', 'dp')
- scale_grad: float32 [8, 448, 2048], P('expert', 'dp')
The draws below stay inside these ranges and needn't reach their ends.
Inputs may be any that keep to these rules, and one draw needn't show every extreme that they name: `expert_index`: the 2 entries of a token name different experts.
All inputs are finite; a program needn't handle non-finite values.
Results may differ from the reference program's by a relative error of at most 0.0058.
Values may be sent and summed in bfloat16 or wider, within the bound.
No kernel may reach another device: no remote copies, remote signals or barrier semaphores. Data moves between devices by JAX's collectives and lax.ppermute only.
A program may use at most 128 MiB of HBM per device.

```python
import math
import jax
import jax.numpy as jnp
from jax import lax

D = 2048
FF = 14336
EXPERTS = 8
TOP = 2
GROUP = 32
TOK_DEV = 512
CAP = 128
TOKENS = 4096
SLOTS = 1024
N_EXPERT = 8


def touch_ends(drawn, key, low, top_value):
    shape = drawn.shape
    place = [jax.random.randint(jax.random.fold_in(key, axis), (), 0, shape[axis]) for axis in range(len(shape))]
    drawn = drawn.at[tuple(place)].set(low)
    longest = shape.index(max(shape))
    place[longest] = (place[longest] + 1) % shape[longest]
    return drawn.at[tuple(place)].set(top_value)


def block_levels(stream_key, shape, pieces, least, largest):
    loudness, own = 1.0, jax.random.fold_in(stream_key, 6)
    for position, blocks in pieces:
        steps = jnp.exp(jax.random.uniform(jax.random.fold_in(own, position), (blocks,), jnp.float32, least / len(pieces), largest / len(pieces)))
        loudness = loudness * jnp.repeat(steps, shape[position] // blocks).reshape([-1 if axis == position else 1 for axis in range(len(shape))])
    return loudness


def different_ones(own_key, rows, count, top, lift):
    order = jax.random.permutation(jax.random.fold_in(own_key, 1), count)
    favour = order
    for power in range(3):
        favour = favour * favour // count
    favour = favour * lift // count
    lots = jax.random.randint(jax.random.fold_in(own_key, 2), (rows, count), 0, 4096) + favour
    fixed_rows = jax.random.permutation(jax.random.fold_in(own_key, 3), rows)[jnp.arange(count) % rows]
    lots = jnp.where(jnp.arange(rows)[:, None] == fixed_rows[None, :], 1 << 14, lots)
    merit = lots * count + jnp.arange(count)
    return lax.top_k(merit.astype(jnp.int32), top)[1].astype(jnp.int32)


def bell_draw(key, dims, deviation, bound, pieces=(), kind=jnp.bfloat16):
    result = jax.random.normal(key, dims, jnp.float32) * deviation
    if len(pieces) > 0:
        result = block_levels(key, dims, pieces, -0.22, 0.18) * result
    return jnp.clip(result, min=-bound, max=bound).astype(kind)


def setup_inputs(seed: int = 0) -> dict:
    keys = jax.random.split(jax.random.key(seed), 7)
    return {
        "hidden": bell_draw(keys[0], (EXPERTS, FF, SLOTS), 1.0, 6.0, ((0, 8), (1, 32))),
        "weight_codes": touch_ends(jax.random.randint(keys[1], (EXPERTS, FF, D), -8, 8), jax.random.fold_in(keys[1], 1), -8, 7).astype(jnp.int32),
        "group_scales": jnp.clip(jnp.exp(math.log(0.0050111483) - 2.014903 * jax.random.uniform(keys[2], (EXPERTS, FF // GROUP, D), jnp.float32) ** block_levels(keys[2], (EXPERTS, FF // GROUP, D), ((0, 8), (1, 32)), -0.2, 0.2)), 0.0006681531, 0.0050111483),
        "expert_index": different_ones(keys[3], TOKENS, EXPERTS, TOP, 4096),
        "gate_values": jnp.clip(0.2 + 0.8 * jax.random.uniform(keys[4], (TOKENS, TOP), jnp.float32) ** block_levels(keys[4], (TOKENS, TOP), ((0, 8),), -0.2, 0.2), 0.2, 1.0),
        "output_grad": bell_draw(keys[5], (TOKENS, D), 1.0, 6.0, ((0, 8), (1, 32))),
    }


def dequantize(codes_one, scales_one):
    grouped = codes_one.astype(jnp.float32).reshape(FF // GROUP, GROUP, D)
    return (grouped * scales_one[:, None, :]).reshape(FF, D).astype(jnp.bfloat16)


def reference(hidden, weight_codes, group_scales, expert_index, gate_values, output_grad):
    group_count = N_EXPERT
    flat_experts = expert_index.reshape(group_count, TOK_DEV * TOP)
    onehot = (flat_experts[:, :, None] == jnp.arange(EXPERTS, dtype=jnp.int32)[None, None, :]).astype(jnp.int32)
    ranking = jnp.sum((jnp.cumsum(onehot, axis=1) - onehot) * onehot, axis=2)
    kept_mask = (ranking < CAP).reshape(TOKENS, TOP)
    group_row = jnp.arange(group_count, dtype=jnp.int32)[:, None]
    slot_index = group_row * CAP + jnp.minimum(ranking, CAP - 1)
    slot_index = slot_index.reshape(TOKENS, TOP).astype(jnp.int32)

    def forward_one(operands):
        hidden_one, codes_one, scales_one = operands
        weight_table = dequantize(codes_one, scales_one)
        return jnp.dot(hidden_one.T, weight_table, preferred_element_type=jnp.float32).astype(jnp.bfloat16)

    expert_out = lax.map(forward_one, (hidden, weight_codes, group_scales))
    gathered = expert_out[expert_index, slot_index].astype(jnp.float32)
    keep_float = kept_mask.astype(jnp.float32)
    weighted = gate_values * keep_float
    grad_float = output_grad.astype(jnp.float32)
    combined = jnp.sum(weighted[:, :, None] * gathered, axis=1).astype(jnp.bfloat16)
    gate_grad = keep_float * jnp.sum(grad_float[:, None, :] * gathered, axis=2)
    values = (weighted[:, :, None] * grad_float[:, None, :]).astype(jnp.bfloat16)
    target = jnp.where(kept_mask, slot_index, SLOTS).astype(jnp.int32)
    slot_grad = jnp.zeros((EXPERTS, SLOTS, D), jnp.bfloat16).at[expert_index, target].set(values, mode="drop")

    def backward_one(operands):
        hidden_one, codes_one, scales_one, grad_one = operands
        weight_table = dequantize(codes_one, scales_one)
        grad_hidden = jnp.dot(weight_table, grad_one.T, preferred_element_type=jnp.float32).astype(jnp.bfloat16)
        grad_weight = jnp.dot(hidden_one, grad_one, preferred_element_type=jnp.float32)
        grad_scale = jnp.sum((grad_weight * codes_one.astype(jnp.float32)).reshape(FF // GROUP, GROUP, D), axis=1)
        return grad_hidden, grad_weight, grad_scale

    hidden_grad, weight_grad, scale_grad = lax.map(backward_one, (hidden, weight_codes, group_scales, slot_grad))
    return combined, gate_grad, hidden_grad, weight_grad, scale_grad
```

```python
import jax
import jax.numpy as jnp
from jax import lax
from jax.experimental import pallas as pl
from jax.experimental.pallas import tpu as pltpu
from jax.sharding import Mesh, PartitionSpec as P

EXPERTS = 8
GROUP = 32
CAP = 128
NY, NC, NX, NZ = 4, 2, 4, 8
COLS = 64
SLOTS = EXPERTS * CAP
PARAMS = pltpu.CompilerParams(vmem_limit_bytes=56 * 1024 * 1024)
F32, BF16, I32 = jnp.float32, jnp.bfloat16, jnp.int32


def sds(shape, dtype):
    return jax.ShapeDtypeStruct(shape, dtype)


def whole(shape):
    return pl.BlockSpec(shape, lambda *_: (0,) * len(shape))


def dequant(codes, scales):
    rows, width = codes.shape
    grouped = codes.astype(F32).reshape(rows // GROUP, GROUP, width)
    return (grouped * scales[:, None, :]).reshape(rows, width).astype(BF16)


def pickers(place_ref):
    lanes = lax.broadcasted_iota(I32, (place_ref.shape[0], SLOTS), 1)
    return [(place_ref[:, k : k + 1] == lanes).astype(BF16) for k in range(2)]


def slot_body(index_ref, gate_ref, grad_ref, place_ref, out_ref):
    tokens = index_ref.shape[0]
    first, second = index_ref[:, 0:1], index_ref[:, 1:2]
    experts = lax.broadcasted_iota(I32, (tokens, 128), 1)
    one_first = (first == experts).astype(F32)
    one_second = (second == experts).astype(F32)
    row = lax.broadcasted_iota(I32, (tokens, tokens), 0)
    col = lax.broadcasted_iota(I32, (tokens, tokens), 1)
    before = (col < row).astype(BF16)
    counts = jnp.dot(before, (one_first + one_second).astype(BF16), preferred_element_type=F32)
    rank_first = jnp.sum(counts * one_first, axis=1, keepdims=True).astype(I32)
    rank_second = jnp.sum(counts * one_second, axis=1, keepdims=True).astype(I32)
    place_ref[:, 0:1] = jnp.where(rank_first < CAP, first * CAP + rank_first, -1)
    place_ref[:, 1:2] = jnp.where(rank_second < CAP, second * CAP + rank_second, -1)
    grad = grad_ref[...].astype(F32)
    total = None
    for k, pick in enumerate(pickers(place_ref)):
        value = (gate_ref[:, k : k + 1] * grad).astype(BF16)
        piece = lax.dot_general(value, pick, (((0,), (0,)), ((), ())), preferred_element_type=F32)
        total = piece if total is None else total + piece
    total = total.astype(BF16)
    for e in range(EXPERTS):
        out_ref[e] = total[:, e * CAP : (e + 1) * CAP]


def slot_grads(index, gate, grad):
    return pl.pallas_call(
        slot_body,
        out_shape=(sds(index.shape, I32), sds((EXPERTS, COLS, CAP), BF16)),
        compiler_params=PARAMS,
        name="slot_grads",
    )(index, gate, grad)


def forward_block(where, k, hidden, codes, scales, types):
    units, slots = hidden.shape
    half = codes.shape[1] // NX // 2
    groups = units // GROUP

    def body(where_ref, hidden_ref, codes_ref, scales_ref, *outs):
        table = dequant(codes_ref[...], scales_ref[...])
        value = lax.dot_general(table, hidden_ref[...], (((0,), (0,)), ((), ())), preferred_element_type=F32)
        for h in range(2):
            @pl.when(pl.program_id(0) == h)
            def _():
                outs[h][...] = value.astype(types[h])

    return pl.pallas_call(
        body,
        grid_spec=pltpu.PrefetchScalarGridSpec(
            num_scalar_prefetch=1,
            grid=(2,),
            in_specs=[
                pl.BlockSpec((units, slots), lambda h, w: (0, 0)),
                pl.BlockSpec((units, half), lambda h, w: (0, lax.rem(w[0] + k, NX) * 2 + h)),
                pl.BlockSpec((groups, half), lambda h, w: (0, lax.rem(w[0] + k, NX) * 2 + h)),
            ],
            out_specs=[pl.BlockSpec((half, slots), lambda h, w: (0, 0)) for _ in range(2)],
        ),
        out_shape=[sds((half, slots), t) for t in types],
        compiler_params=PARAMS,
        name=f"forward_{k}",
    )(where, hidden, codes, scales)


def x_sum_body(where_ref, top, bottom, top_a, top_b, bottom_a, bottom_b, *outs):
    z = where_ref[1]
    acc_top = top[...] + top_a[...].astype(F32) + top_b[...].astype(F32)
    acc_bottom = bottom[...] + bottom_a[...].astype(F32) + bottom_b[...].astype(F32)
    scratch = outs[-1]
    half = acc_top.shape[0]
    scratch[:half] = acc_top
    scratch[half:] = acc_bottom
    for k in range(NZ):
        start = pl.multiple_of(lax.rem(z + k, NZ) * COLS, COLS)
        outs[k][...] = scratch[pl.ds(start, COLS), :].astype(outs[k].dtype)


def x_sum(where, *arrays):
    half, slots = arrays[0].shape
    kinds = [F32, BF16, F32, BF16, BF16, BF16, F32, BF16]
    return pl.pallas_call(
        x_sum_body,
        grid_spec=pltpu.PrefetchScalarGridSpec(
            num_scalar_prefetch=1,
            grid=(1,),
            in_specs=[whole((half, slots)) for _ in arrays],
            out_specs=[whole((COLS, slots)) for _ in kinds],
            scratch_shapes=[pltpu.VMEM((2 * half, slots), F32)],
        ),
        out_shape=[sds((COLS, slots), t) for t in kinds],
        compiler_params=PARAMS,
        name="x_sum",
    )(where, *arrays)


def z_sum_body(own, *rest):
    total = own[...]
    for piece in rest[:-1]:
        total = total + piece[...].astype(F32)
    total = total.astype(BF16)
    for g in range(EXPERTS):
        rest[-1][g] = total[:, g * CAP : (g + 1) * CAP]


def z_sum(*arrays):
    return pl.pallas_call(
        z_sum_body, out_shape=sds((EXPERTS, COLS, CAP), BF16), compiler_params=PARAMS, name="z_sum"
    )(*arrays)


def combine_body(place_ref, gate_ref, grad_ref, back_ref, out_ref, gate_out_ref):
    back = jnp.concatenate([back_ref[e] for e in range(EXPERTS)], axis=1)
    grad = grad_ref[...].astype(F32)
    total = None
    ones = jnp.ones((8, COLS), F32)
    for k, pick in enumerate(pickers(place_ref)):
        got = lax.dot_general(pick, back, (((1,), (1,)), ((), ())), preferred_element_type=F32)
        piece = gate_ref[:, k : k + 1] * got
        total = piece if total is None else total + piece
        sums = lax.dot_general(
            ones, grad * got, (((1,), (1,)), ((), ())), preferred_element_type=F32, precision=lax.Precision.HIGHEST
        )
        for j in range(4):
            gate_out_ref[k * 4 + j : k * 4 + j + 1, :] = sums[0:1, j * 128 : (j + 1) * 128]
    out_ref[...] = total.astype(BF16)


def combine(place, gate, grad, back):
    return pl.pallas_call(
        combine_body,
        out_shape=(sds(grad.shape, BF16), sds((8, 128), F32)),
        compiler_params=PARAMS,
        name="combine",
    )(place, gate, grad, back)


def gate_sum_body(parts_ref, out_ref):
    total = jnp.sum(parts_ref[...], axis=0)
    turned = total.T
    for j in range(4):
        out_ref[j * 128 : (j + 1) * 128, 0:1] = turned[:, j : j + 1]
        out_ref[j * 128 : (j + 1) * 128, 1:2] = turned[:, 4 + j : 5 + j]


def gate_sum(parts):
    return pl.pallas_call(
        gate_sum_body, out_shape=sds((512, 2), F32), compiler_params=PARAMS, name="gate_sum"
    )(parts)


STEPS = 4


def backward_body(where_ref, hidden_ref, codes_ref, scales_ref, *rest):
    owns, trios = rest[:NZ], rest[NZ : 2 * NZ]
    hidden_out, weight_out, scale_out, grads, acc = rest[2 * NZ :]
    step = pl.program_id(0)
    x, z = where_ref[0], where_ref[1]

    @pl.when(step == 0)
    def _():
        for k in range(NZ):
            for i, dx in enumerate((0, 1, 3, 2)):
                owner = lax.rem(x + dx, NX) * NZ + lax.rem(z + k, NZ)
                start = pl.multiple_of(owner * COLS, COLS)
                for g in range(EXPERTS):
                    piece = owns[k][g] if i == 0 else trios[k][i - 1, g]
                    grads[pl.ds(start, COLS), g * CAP : (g + 1) * CAP] = piece

    width = codes_ref.shape[1]
    codes = codes_ref[...]
    table = dequant(codes, scales_ref[...])
    block = grads[pl.ds(pl.multiple_of(step * width, width), width), :]
    part = jnp.dot(table, block, preferred_element_type=F32)

    @pl.when(step == 0)
    def _():
        acc[...] = part

    @pl.when(jnp.logical_and(step > 0, step < STEPS - 1))
    def _():
        acc[...] = acc[...] + part

    @pl.when(step == STEPS - 1)
    def _():
        hidden_out[...] = (acc[...] + part).astype(BF16)

    weight = lax.dot_general(hidden_ref[...], block, (((1,), (1,)), ((), ())), preferred_element_type=F32)
    weight_out[...] = weight
    products = weight * codes.astype(F32)
    scale_out[...] = jnp.sum(products.reshape(-1, GROUP, width), axis=1)


def backward(where, hidden, codes, scales, owns, trios):
    units, slots = hidden.shape
    features = codes.shape[1]
    width = features // STEPS
    groups = units // GROUP
    return pl.pallas_call(
        backward_body,
        grid_spec=pltpu.PrefetchScalarGridSpec(
            num_scalar_prefetch=1,
            grid=(STEPS,),
            in_specs=[
                whole((units, slots)),
                pl.BlockSpec((units, width), lambda n, w: (0, n)),
                pl.BlockSpec((groups, width), lambda n, w: (0, n)),
            ]
            + [whole(a.shape) for a in owns]
            + [whole(a.shape) for a in trios],
            out_specs=[
                whole((units, slots)),
                pl.BlockSpec((units, width), lambda n, w: (0, n)),
                pl.BlockSpec((groups, width), lambda n, w: (0, n)),
            ],
            scratch_shapes=[pltpu.VMEM((features, slots), BF16), pltpu.VMEM((units, slots), F32)],
        ),
        out_shape=[sds((units, slots), BF16), sds((units, features), F32), sds((groups, features), F32)],
        compiler_params=PARAMS,
        name="backward",
    )(where, hidden, codes, scales, *owns, *trios)


def shift(value, axis, by):
    size = NX if axis == "x" else NZ
    return lax.ppermute(value, axis, [(i, (i + by) % size) for i in range(size)])


def to_experts(value):
    return lax.all_to_all(value, ("y", "c"), 0, 0, tiled=True)


def on_device(hidden, weight_codes, group_scales, expert_index, gate_values, output_grad):
    hidden, codes, scales = hidden[0], weight_codes[0], group_scales[0]
    where = jnp.stack([lax.axis_index("x"), lax.axis_index("z")]).astype(I32)

    far_top, far_bottom = forward_block(where, 2, hidden, codes, scales, (BF16, BF16))
    far_top = shift(far_top, "x", 1)
    far_bottom = shift(far_bottom, "x", -1)
    place, outbound = slot_grads(expert_index, gate_values, output_grad)
    shard = to_experts(outbound)
    up_top, up_bottom = forward_block(where, 1, hidden, codes, scales, (F32, BF16))
    down_top, down_bottom = forward_block(where, 3, hidden, codes, scales, (BF16, F32))
    own_top, own_bottom = forward_block(where, 0, hidden, codes, scales, (F32, F32))
    bottom_a = shift(up_bottom, "x", 1)
    top_a = shift(down_top, "x", -1)
    top_b = shift((up_top + far_top.astype(F32)).astype(BF16), "x", 1)
    bottom_b = shift((down_bottom + far_bottom.astype(F32)).astype(BF16), "x", -1)

    trio = jnp.stack([shift(shard, "x", -1), shift(shard, "x", 1), shift(shard, "x", 2)])
    owns, trios = {0: shard}, {0: trio}
    for hop in range(1, 5):
        owns[NZ - hop] = shift(owns[(NZ - hop + 1) % NZ], "z", 1)
        if hop < 4:
            owns[hop] = shift(owns[hop - 1], "z", -1)
    for hop in range(1, 5):
        trios[hop] = shift(trios[hop - 1], "z", -1)
        if hop < 4:
            trios[NZ - hop] = shift(trios[(NZ - hop + 1) % NZ], "z", 1)

    own, up1, up2, up3, up4, down3, down2, down1 = x_sum(
        where, own_top, own_bottom, top_a, top_b, bottom_a, bottom_b
    )
    got4 = shift(up4, "z", 2)
    got3 = shift(up3, "z", 1)
    gotm3 = shift(down3, "z", -1)
    got1 = shift(up1, "z", 1)
    gotm1 = shift(down1, "z", -1)
    got2 = shift((up2 + got3.astype(F32) + got4.astype(F32)).astype(BF16), "z", 2)
    gotm2 = shift((down2 + gotm3.astype(F32)).astype(BF16), "z", -2)
    outgoing = z_sum(own, got1, got2, gotm1, gotm2)
    returned = to_experts(outgoing)
    combined, gate_part = combine(place, gate_values, output_grad, returned)
    spread = jnp.broadcast_to(gate_part[None], (NX * NZ, 8, 128))
    gate_grad = gate_sum(lax.all_to_all(spread, ("x", "z"), 0, 0, tiled=True))

    hidden_grad, weight_grad, scale_grad = backward(
        where, hidden, codes, scales, [owns[k] for k in range(NZ)], [trios[k] for k in range(NZ)]
    )
    return combined, gate_grad, hidden_grad[None], weight_grad[None], scale_grad[None]


def solution(mesh):
    fine = Mesh(mesh.devices.reshape(NY, NC, NX, NZ), ("y", "c", "x", "z"))
    expert, dp = ("y", "c"), ("x", "z")
    return jax.shard_map(
        on_device,
        mesh=fine,
        in_specs=(
            P(expert, dp, None),
            P(expert, dp, None),
            P(expert, dp, None),
            P(expert, None),
            P(expert, None),
            P(expert, dp),
        ),
        out_specs=(
            P(expert, dp),
            P(expert, None),
            P(expert, dp, None),
            P(expert, dp, None),
            P(expert, dp, None),
        ),
        check_vma=False,
    )
```

```python
import jax
import jax.numpy as jnp
from jax import lax
from jax.experimental import pallas as pl
from jax.experimental.pallas import tpu as pltpu
from jax.sharding import Mesh, PartitionSpec as P

EXPERTS = 8
GROUP = 32
CAP = 128
NY, NC, NX, NZ = 4, 2, 4, 8
COLS = 64
SLOTS = EXPERTS * CAP
BLOCK = NZ * COLS
PARAMS = pltpu.CompilerParams(vmem_limit_bytes=56 * 1024 * 1024)
F32, BF16, I32 = jnp.float32, jnp.bfloat16, jnp.int32


def sds(shape, dtype):
    return jax.ShapeDtypeStruct(shape, dtype)


def whole(shape):
    return pl.BlockSpec(shape, lambda *_: (0,) * len(shape))


def dequant(codes, scales):
    rows, width = codes.shape
    grouped = codes.astype(F32).reshape(rows // GROUP, GROUP, width)
    return (grouped * scales[:, None, :]).reshape(rows, width).astype(BF16)


def picker(place_ref, k):
    slots = lax.broadcasted_iota(I32, (SLOTS, place_ref.shape[1]), 0)
    return (place_ref[k : k + 1, :] == slots).astype(BF16)


def slot_body(index_ref, gate_ref, grad_ref, place_ref, out_ref):
    tokens = index_ref.shape[1]
    experts = lax.broadcasted_iota(I32, (EXPERTS, tokens), 0)
    hot = [(index_ref[k : k + 1, :] == experts).astype(F32) for k in range(2)]
    row = lax.broadcasted_iota(I32, (tokens, tokens), 0)
    col = lax.broadcasted_iota(I32, (tokens, tokens), 1)
    before = (row < col).astype(BF16)
    counts = jnp.dot((hot[0] + hot[1]).astype(BF16), before, preferred_element_type=F32)
    for k in range(2):
        rank = jnp.sum(counts * hot[k], axis=0, keepdims=True).astype(I32)
        place_ref[k : k + 1, :] = jnp.where(rank < CAP, index_ref[k : k + 1, :] * CAP + rank, -1)
    grad = grad_ref[...].astype(F32)
    total = None
    for k in range(2):
        value = (gate_ref[k : k + 1, :] * grad).astype(BF16)
        piece = lax.dot_general(
            value, picker(place_ref, k), (((1,), (1,)), ((), ())), preferred_element_type=F32
        )
        total = piece if total is None else total + piece
    total = total.astype(BF16)
    for e in range(EXPERTS):
        for x in range(NX):
            out_ref[e * NX + x] = total[:, e * CAP : (e + 1) * CAP]


def slot_grads(index, gate, grad):
    return pl.pallas_call(
        slot_body,
        out_shape=(sds(index.shape, I32), sds((EXPERTS * NX, COLS, CAP), BF16)),
        compiler_params=PARAMS,
        name="slot_grads",
    )(index, gate, grad)


def forward_body(where_ref, hidden_ref, codes_ref, scales_ref, out_ref):
    table = dequant(codes_ref[...], scales_ref[...])
    value = lax.dot_general(table, hidden_ref[...], (((0,), (0,)), ((), ())), preferred_element_type=F32)
    out_ref[0] = value.astype(out_ref.dtype)


def forward(where, hidden, codes, scales, far):
    units, slots = hidden.shape
    count = 1 if far else 3
    half = BLOCK // 2

    def block(n, w):
        away = 2 if far else lax.rem(2 * (n // 2) + 1, 5)
        return (0, lax.rem(w[0] + away, NX) * 2 + lax.rem(n, 2))

    return pl.pallas_call(
        forward_body,
        grid_spec=pltpu.PrefetchScalarGridSpec(
            num_scalar_prefetch=1,
            grid=(count * 2,),
            in_specs=[
                pl.BlockSpec((units, slots), lambda n, w: (0, 0)),
                pl.BlockSpec((units, half), block),
                pl.BlockSpec((units // GROUP, half), block),
            ],
            out_specs=pl.BlockSpec((1, half, slots), lambda n, w: (n, 0, 0)),
        ),
        out_shape=sds((count * 2, half, slots), BF16 if far else F32),
        compiler_params=PARAMS,
        name="forward_far" if far else "forward_near",
    )(where, hidden, codes, scales)


def join_body(near_ref, top_ref, bottom_ref, up_ref, down_ref):
    half = BLOCK // 2
    up_ref[:half] = (near_ref[0] + top_ref[...].astype(F32)).astype(BF16)
    up_ref[half:] = near_ref[1].astype(BF16)
    down_ref[:half] = near_ref[2].astype(BF16)
    down_ref[half:] = (near_ref[3] + bottom_ref[...].astype(F32)).astype(BF16)


def join(near, top, bottom):
    half, slots = top.shape
    return pl.pallas_call(
        join_body,
        grid=(1,),
        in_specs=[pl.BlockSpec((4, half, slots), lambda n: (0, 0, 0)), whole(top.shape), whole(top.shape)],
        out_specs=[whole((2 * half, slots))] * 2,
        out_shape=[sds((2 * half, slots), BF16)] * 2,
        compiler_params=PARAMS,
        name="join",
    )(near, top, bottom)


def x_sum_body(near_ref, up_ref, down_ref, out_ref):
    half = BLOCK // 2
    for z in range(NZ):
        rows = slice(z * COLS, (z + 1) * COLS)
        h, r = divmod(z * COLS, half)
        total = near_ref[h, r : r + COLS, :] + up_ref[rows, :].astype(F32) + down_ref[rows, :].astype(F32)
        total = total.astype(BF16)
        for g in range(EXPERTS):
            out_ref[z * EXPERTS + g] = total[:, g * CAP : (g + 1) * CAP]


def x_sum(near, up, down):
    rows, slots = up.shape
    return pl.pallas_call(
        x_sum_body,
        grid=(1,),
        in_specs=[pl.BlockSpec((2, rows // 2, slots), lambda n: (2, 0, 0)), whole(up.shape), whole(up.shape)],
        out_specs=whole((NZ * EXPERTS, COLS, CAP)),
        out_shape=sds((NZ * EXPERTS, COLS, CAP), BF16),
        compiler_params=PARAMS,
        name="x_sum",
    )(near, up, down)


def combine_body(place_ref, gate_ref, grad_ref, back_ref, out_ref, spread_ref):
    sums = []
    for e in range(EXPERTS):
        total = back_ref[e].astype(F32)
        for z in range(1, NZ):
            total = total + back_ref[z * EXPERTS + e].astype(F32)
        sums.append(total.astype(BF16))
    back = jnp.concatenate(sums, axis=1)
    grad = grad_ref[...].astype(F32)
    total = None
    for k in range(2):
        got = jnp.dot(back, picker(place_ref, k), preferred_element_type=F32)
        piece = gate_ref[k : k + 1, :] * got
        total = piece if total is None else total + piece
        part = jnp.sum(grad * got, axis=0, keepdims=True)
        for j in range(4):
            line = part[:, j * 128 : (j + 1) * 128]
            spread_ref[:, k * 4 + j : k * 4 + j + 1, :] = jnp.broadcast_to(line[None], (NX * NZ, 1, 128))
    out_ref[...] = total.astype(BF16)


def combine(place, gate, grad, back):
    return pl.pallas_call(
        combine_body,
        out_shape=(sds(grad.shape, BF16), sds((NX * NZ, 8, 128), F32)),
        compiler_params=PARAMS,
        name="combine",
    )(place, gate, grad, back)


def gate_sum_body(parts_ref, out_ref):
    total = jnp.sum(parts_ref[...], axis=0)
    for k in range(2):
        for j in range(4):
            out_ref[k : k + 1, j * 128 : (j + 1) * 128] = total[k * 4 + j : k * 4 + j + 1, :]


def gate_sum(parts):
    return pl.pallas_call(
        gate_sum_body, out_shape=sds((2, 512), F32), compiler_params=PARAMS, name="gate_sum"
    )(parts)


def backward_body(hidden_ref, codes_ref, scales_ref, grads_ref, hidden_out, weight_out, scale_out, acc):
    step = pl.program_id(0)
    width = codes_ref.shape[1]
    block = jnp.concatenate(
        [jnp.concatenate([grads_ref[z, g, 0] for g in range(EXPERTS)], axis=1) for z in range(NZ)], axis=0
    )
    codes = codes_ref[...]
    part = jnp.dot(dequant(codes, scales_ref[...]), block, preferred_element_type=F32)

    @pl.when(step == 0)
    def _():
        acc[...] = part

    @pl.when(jnp.logical_and(step > 0, step < NX - 1))
    def _():
        acc[...] = acc[...] + part

    @pl.when(step == NX - 1)
    def _():
        hidden_out[...] = (acc[...] + part).astype(BF16)

    weight = lax.dot_general(hidden_ref[...], block, (((1,), (1,)), ((), ())), preferred_element_type=F32)
    weight_out[...] = weight
    products = weight * codes.astype(F32)
    scale_out[...] = jnp.sum(products.reshape(-1, GROUP, width), axis=1)


def backward(hidden, codes, scales, grads):
    units, slots = hidden.shape
    features = codes.shape[1]
    groups = units // GROUP
    return pl.pallas_call(
        backward_body,
        grid=(NX,),
        in_specs=[
            whole((units, slots)),
            pl.BlockSpec((units, BLOCK), lambda n: (0, n)),
            pl.BlockSpec((groups, BLOCK), lambda n: (0, n)),
            pl.BlockSpec((NZ, EXPERTS, 1, COLS, CAP), lambda n: (0, 0, n, 0, 0)),
        ],
        out_specs=[
            whole((units, slots)),
            pl.BlockSpec((units, BLOCK), lambda n: (0, n)),
            pl.BlockSpec((groups, BLOCK), lambda n: (0, n)),
        ],
        out_shape=[sds((units, slots), BF16), sds((units, features), F32), sds((groups, features), F32)],
        scratch_shapes=[pltpu.VMEM((units, slots), F32)],
        compiler_params=PARAMS,
        name="backward",
    )(hidden, codes, scales, grads)


def shift(value, axis, by):
    size = NX if axis == "x" else NZ
    return lax.ppermute(value, axis, [(i, (i + by) % size) for i in range(size)])


def on_device(hidden, weight_codes, group_scales, expert_index, gate_values, output_grad):
    hidden, codes, scales = hidden[0], weight_codes[0], group_scales[0]
    index, gate, grad = expert_index.T, gate_values.T, output_grad.T
    where = lax.axis_index("x").astype(I32).reshape(1)

    far = forward(where, hidden, codes, scales, True)
    far_top = shift(far[0], "x", 1)
    far_bottom = shift(far[1], "x", -1)

    place, outbound = slot_grads(index, gate, grad)
    shard = lax.all_to_all(outbound, ("y", "c", "x"), 0, 0, tiled=True)
    gathered = lax.all_gather(shard.reshape(EXPERTS * NX * COLS, CAP), "z", axis=0, tiled=True)

    near = forward(where, hidden, codes, scales, False)
    up, down = join(near, far_top, far_bottom)
    up = shift(up, "x", 1)
    down = shift(down, "x", -1)

    returned = lax.all_to_all(x_sum(near, up, down), ("z", "y", "c"), 0, 0, tiled=True)
    combined, spread = combine(place, gate, grad, returned)
    gate_grad = gate_sum(lax.all_to_all(spread, ("x", "z"), 0, 0, tiled=True))

    grads = gathered.reshape(NZ, EXPERTS, NX, COLS, CAP)
    hidden_grad, weight_grad, scale_grad = backward(hidden, codes, scales, grads)
    return combined.T, gate_grad.T, hidden_grad[None], weight_grad[None], scale_grad[None]


def solution(mesh):
    fine = Mesh(mesh.devices.reshape(NY, NC, NX, NZ), ("y", "c", "x", "z"))
    expert, dp = ("y", "c"), ("x", "z")
    return jax.shard_map(
        on_device,
        mesh=fine,
        in_specs=(
            P(expert, dp, None),
            P(expert, dp, None),
            P(expert, dp, None),
            P(expert, None),
            P(expert, None),
            P(expert, dp),
        ),
        out_specs=(
            P(expert, dp),
            P(expert, None),
            P(expert, dp, None),
            P(expert, dp, None),
            P(expert, dp, None),
        ),
        check_vma=False,
    )
```

```python
import jax
import jax.numpy as jnp
from jax import lax
from jax.experimental import pallas as pl
from jax.experimental.pallas import tpu as pltpu
from jax.sharding import Mesh, PartitionSpec as P

EXPERTS = 8
GROUP = 32
CAP = 128
NY, NC, NX, NZ = 4, 2, 4, 8
COLS = 64
SLOTS = EXPERTS * CAP
BLOCK = NZ * COLS
SMALL = pltpu.CompilerParams(vmem_limit_bytes=16 * 1024 * 1024)
LARGE = pltpu.CompilerParams(vmem_limit_bytes=32 * 1024 * 1024)
F32, BF16, I32 = jnp.float32, jnp.bfloat16, jnp.int32


sds = jax.ShapeDtypeStruct
HBM, VMEM, SMEM = (pl.BlockSpec(memory_space=m) for m in (pltpu.HBM, pltpu.VMEM, pltpu.SMEM))


def near(array):
    return pltpu.with_memory_space_constraint(array, pltpu.VMEM)


def away(array):
    return pltpu.with_memory_space_constraint(array, pltpu.HBM)


def call(body, name, where, operands, outs, scratch=(), far=()):
    heads = [] if where is None else [where]
    return pl.pallas_call(
        body,
        in_specs=[SMEM] * len(heads) + [HBM] * len(far) + [VMEM] * len(operands),
        out_specs=[VMEM] * len(outs),
        out_shape=[pltpu.VMEM(shape, dtype) for shape, dtype in outs],
        scratch_shapes=list(scratch),
        compiler_params=SMALL,
        name=name,
    )(*heads, *[away(a) for a in far], *[near(a) for a in operands])


def dequant(codes_ref, scales_ref, tile, table_ref):
    units, width = codes_ref.shape
    tiles = scales_ref.shape[0] // (units // GROUP)
    for j in range(width // 128):
        lanes = slice(j * 128, (j + 1) * 128)
        for g in range(units // GROUP):
            rows = slice(g * GROUP, (g + 1) * GROUP)
            scale = scales_ref[pl.ds(g * tiles + tile + j, 1), :]
            table_ref[rows, lanes] = (codes_ref[rows, lanes].astype(F32) * scale).astype(BF16)


def picker(place_ref, k):
    slots = lax.broadcasted_iota(I32, (SLOTS, place_ref.shape[1]), 0)
    return (place_ref[k : k + 1, :] == slots).astype(BF16)


def slot_body(index_ref, gate_ref, grad_ref, place_ref, out_ref):
    tokens = index_ref.shape[1]
    experts = lax.broadcasted_iota(I32, (EXPERTS, tokens), 0)
    hot = [(index_ref[k : k + 1, :] == experts).astype(F32) for k in range(2)]
    row = lax.broadcasted_iota(I32, (tokens, tokens), 0)
    col = lax.broadcasted_iota(I32, (tokens, tokens), 1)
    before = (row < col).astype(BF16)
    counts = jnp.dot((hot[0] + hot[1]).astype(BF16), before, preferred_element_type=F32)
    for k in range(2):
        rank = jnp.sum(counts * hot[k], axis=0, keepdims=True).astype(I32)
        place_ref[k : k + 1, :] = jnp.where(rank < CAP, index_ref[k : k + 1, :] * CAP + rank, -1)
    grad = grad_ref[...].astype(F32)
    total = None
    for k in range(2):
        value = (gate_ref[k : k + 1, :] * grad).astype(BF16)
        piece = lax.dot_general(
            value, picker(place_ref, k), (((1,), (1,)), ((), ())), preferred_element_type=F32
        )
        total = piece if total is None else total + piece
    total = total.astype(BF16)
    for e in range(EXPERTS):
        for x in range(NX):
            out_ref[e * NX + x] = total[:, e * CAP : (e + 1) * CAP]


def slot_grads(index, gate, grad):
    outs = [(index.shape, I32), ((EXPERTS * NX, COLS, CAP), BF16)]
    return call(slot_body, "slot_grads", None, [index, gate, grad], outs)


def loads(where_ref, hops, hidden_hbm, codes_hbm, scales_hbm, hidden, codes, scales, sems):
    copies = [
        pltpu.make_async_copy(scales_hbm, scales, sems.at[0]),
        pltpu.make_async_copy(hidden_hbm, hidden, sems.at[1]),
    ]
    for i, hop in enumerate(hops):
        start = pl.multiple_of(lax.rem(where_ref[0] + hop, NX) * BLOCK, BLOCK)
        copies.append(pltpu.make_async_copy(codes_hbm.at[:, pl.ds(start, BLOCK)], codes.at[i], sems.at[2 + i]))
    for copy in copies:
        copy.start()
    copies[0].wait()
    return copies[1:]


def buffers(units, count):
    return [
        pltpu.VMEM((units, SLOTS), BF16),
        pltpu.VMEM((count, units, BLOCK), I32),
        pltpu.VMEM((units // GROUP * (NX * BLOCK // 128), 128), F32),
        pltpu.VMEM((units, BLOCK), BF16),
        pltpu.SemaphoreType.DMA((2 + count,)),
    ]


def block_value(where_ref, hops, hidden, codes, scales, table, copy, others=()):
    copy.wait()
    dequant(codes, scales, lax.rem(where_ref[0] + hops, NX) * (BLOCK // 128), table)
    for other in others:
        other.wait()
    return lax.dot_general(table[...], hidden[...], (((0,), (0,)), ((), ())), preferred_element_type=F32)


def far_body(where_ref, hidden_hbm, codes_hbm, scales_hbm, top_ref, bottom_ref, hidden, codes, scales, table, sems):
    first, *copies = loads(where_ref, (2,), hidden_hbm, codes_hbm, scales_hbm, hidden, codes, scales, sems)
    value = block_value(where_ref, 2, hidden, codes.at[0], scales, table, copies[0], (first,)).astype(BF16)
    top_ref[...] = value[: BLOCK // 2]
    bottom_ref[...] = value[BLOCK // 2 :]


def forward_far(where, *arrays):
    half = ((BLOCK // 2, SLOTS), BF16)
    return call(far_body, "forward_far", where, [], [half, half], buffers(arrays[0].shape[0], 1), arrays)


def join_body(
    where_ref, hidden_hbm, codes_hbm, scales_hbm, top_ref, bottom_ref, up_ref, down_ref, hidden, codes, scales, table, sems
):
    first, *copies = loads(where_ref, (1, 3), hidden_hbm, codes_hbm, scales_hbm, hidden, codes, scales, sems)
    half = BLOCK // 2
    value = block_value(where_ref, 1, hidden, codes.at[0], scales, table, copies[0], (first,))
    up_ref[:half] = (value[:half] + top_ref[...].astype(F32)).astype(BF16)
    up_ref[half:] = value[half:].astype(BF16)
    value = block_value(where_ref, 3, hidden, codes.at[1], scales, table, copies[1])
    down_ref[:half] = value[:half].astype(BF16)
    down_ref[half:] = (value[half:] + bottom_ref[...].astype(F32)).astype(BF16)


def forward_join(where, hidden, codes, scales, top, bottom):
    outs = [((BLOCK, SLOTS), BF16)] * 2
    far = (hidden, codes, scales)
    return call(join_body, "forward_join", where, [top, bottom], outs, buffers(hidden.shape[0], 2), far)


def own_body(where_ref, hidden_hbm, codes_hbm, scales_hbm, own_ref, hidden, codes, scales, table, sems):
    first, *copies = loads(where_ref, (0,), hidden_hbm, codes_hbm, scales_hbm, hidden, codes, scales, sems)
    own_ref[...] = block_value(where_ref, 0, hidden, codes.at[0], scales, table, copies[0], (first,))


def forward_own(where, *arrays):
    outs = [((BLOCK, SLOTS), F32)]
    return call(own_body, "forward_own", where, [], outs, buffers(arrays[0].shape[0], 1), arrays)[0]


def x_sum_body(own_ref, up_ref, down_ref, out_ref):
    for z in range(NZ):
        rows = slice(z * COLS, (z + 1) * COLS)
        total = own_ref[rows, :] + up_ref[rows, :].astype(F32) + down_ref[rows, :].astype(F32)
        out_ref[z] = total.astype(BF16)


def x_sum(*arrays):
    return call(x_sum_body, "x_sum", None, arrays, [((NZ, COLS, SLOTS), BF16)])[0]


def z_sum_body(parts_ref, out_ref):
    total = parts_ref[0].astype(F32)
    for z in range(1, NZ):
        total = total + parts_ref[z].astype(F32)
    total = total.astype(BF16)
    for g in range(EXPERTS):
        out_ref[g] = total[:, g * CAP : (g + 1) * CAP]


def z_sum(parts):
    return call(z_sum_body, "z_sum", None, [parts], [((EXPERTS, COLS, CAP), BF16)])[0]


def combine_body(place_ref, gate_ref, grad_ref, back_ref, out_ref, spread_ref):
    back = jnp.concatenate([back_ref[e] for e in range(EXPERTS)], axis=1)
    grad = grad_ref[...].astype(F32)
    total = None
    for k in range(2):
        got = jnp.dot(back, picker(place_ref, k), preferred_element_type=F32)
        piece = gate_ref[k : k + 1, :] * got
        total = piece if total is None else total + piece
        part = jnp.sum(grad * got, axis=0, keepdims=True)
        for j in range(4):
            line = part[:, j * 128 : (j + 1) * 128]
            spread_ref[:, k * 4 + j : k * 4 + j + 1, :] = jnp.broadcast_to(line[None], (NX * NZ, 1, 128))
    out_ref[...] = total.astype(BF16)


def combine(place, gate, grad, back):
    outs = [(grad.shape, BF16), ((NX * NZ, 8, 128), F32)]
    return call(combine_body, "combine", None, [place, gate, grad, back], outs)


def gate_sum_body(parts_ref, out_ref):
    total = jnp.sum(parts_ref[...], axis=0)
    for k in range(2):
        for j in range(4):
            out_ref[k : k + 1, j * 128 : (j + 1) * 128] = total[k * 4 + j : k * 4 + j + 1, :]


def gate_sum(parts):
    return call(gate_sum_body, "gate_sum", None, [parts], [((2, 512), F32)])[0]


def backward_body(where_ref, hidden_hbm, codes_hbm, scales_hbm, *rest):
    pieces = rest[:NZ]
    hidden_out, weight_out, scale_out = rest[NZ : NZ + 3]
    hidden, codes, scales, grads, table, weight, sems = rest[NZ + 3 :]
    units = hidden.shape[0]
    tiles = BLOCK // 128
    head = [
        pltpu.make_async_copy(hidden_hbm, hidden, sems.at[0]),
        pltpu.make_async_copy(scales_hbm, scales, sems.at[1]),
    ]
    parts, arrive = [], []
    for n in range(NX):
        lanes = slice(n * BLOCK, (n + 1) * BLOCK)
        parts.append(pltpu.make_async_copy(codes_hbm.at[:, lanes], codes.at[n], sems.at[2 + n]))
        arrive.append([])
        for k in range(NZ):
            z = lax.rem(where_ref[1] + k, NZ)
            rows = pl.ds(pl.multiple_of(n * BLOCK + z * COLS, COLS), COLS)
            arrive[n].append(pltpu.make_async_copy(pieces[k].at[:, n], grads.at[:, rows], sems.at[8 + n * NZ + k]))
    head[0].start()
    for copy in arrive[0]:
        copy.start()
    head[1].start()
    parts[0].start()
    for n in range(1, NX):
        for copy in arrive[n]:
            copy.start()
        parts[n].start()
    head[0].wait()
    head[1].wait()
    copies = []
    for n in range(NX):
        lanes = slice(n * BLOCK, (n + 1) * BLOCK)
        for copy in arrive[n]:
            copy.wait()
        block = jnp.concatenate([grads[g, lanes, :] for g in range(EXPERTS)], axis=1)
        slot = n % 2
        if n >= 2:
            copies[n - 2].wait()
        weight[slot] = lax.dot_general(
            hidden[...], block, (((1,), (1,)), ((), ())), preferred_element_type=F32
        )
        copies.append(pltpu.make_async_copy(weight.at[slot], weight_out.at[:, lanes], sems.at[6 + slot]))
        copies[n].start()
        parts[n].wait()
        dequant(codes.at[n], scales, n * tiles, table.at[:, lanes])
        for g in range(units // GROUP):
            rows = slice(g * GROUP, (g + 1) * GROUP)
            line = jnp.sum(weight[slot, rows, :] * codes[n, rows, :].astype(F32), axis=0, keepdims=True)
            for j in range(tiles):
                row = (g * NX + n) * tiles + j
                scale_out[row : row + 1, :] = line[:, j * 128 : (j + 1) * 128]
    block = jnp.concatenate([grads[g] for g in range(EXPERTS)], axis=1)
    hidden_out[...] = jnp.dot(table[...], block, preferred_element_type=F32).astype(BF16)
    copies[2].wait()
    copies[3].wait()


def backward(where, hidden, codes, scales, pieces):
    units, slots = hidden.shape
    features = codes.shape[1]
    pieces = [a.reshape(EXPERTS, NX, COLS, CAP) for a in pieces]
    return pl.pallas_call(
        backward_body,
        in_specs=[SMEM] + [HBM] * (3 + NZ),
        out_specs=[VMEM, HBM, VMEM],
        out_shape=[sds((units, slots), BF16), sds((units, features), F32), sds(scales.shape, F32)],
        scratch_shapes=[
            pltpu.VMEM((units, slots), BF16),
            pltpu.VMEM((NX, units, BLOCK), I32),
            pltpu.VMEM(scales.shape, F32),
            pltpu.VMEM((EXPERTS, features, CAP), BF16),
            pltpu.VMEM((units, features), BF16),
            pltpu.VMEM((2, units, BLOCK), F32),
            pltpu.SemaphoreType.DMA((8 + NX * NZ,)),
        ],
        compiler_params=LARGE,
        name="backward",
    )(where, *[away(a) for a in (hidden, codes, scales, *pieces)])


def shift(value, axis, by):
    size = NX if axis == "x" else NZ
    return lax.ppermute(value, axis, [(i, (i + by) % size) for i in range(size)])


def on_device(hidden, weight_codes, group_scales, expert_index, gate_values, output_grad):
    weights = (hidden[0], weight_codes[0], group_scales.reshape(-1, 128))
    index, gate, grad = expert_index.T, gate_values.T, output_grad.T
    where = jnp.stack([lax.axis_index("x"), lax.axis_index("z")]).astype(I32)

    far_top, far_bottom = forward_far(where, *weights)
    far_top = shift(far_top, "x", 1)
    far_bottom = shift(far_bottom, "x", -1)

    place, outbound = slot_grads(index, gate, grad)
    pieces = {0: lax.all_to_all(outbound, ("y", "c", "x"), 0, 0, tiled=True)}

    def turn(hop):
        pieces[hop] = shift(pieces[hop - 1], "z", -1)
        if hop < 4:
            pieces[NZ - hop] = shift(pieces[(NZ - hop + 1) % NZ], "z", 1)

    far_top, far_bottom, pieces[0] = lax.optimization_barrier((far_top, far_bottom, pieces[0]))
    up, down = forward_join(where, *weights, far_top, far_bottom)
    where_late, up, down = lax.optimization_barrier((where, up, down))
    up = shift(up, "x", 1)
    down = shift(down, "x", -1)
    own = forward_own(where_late, *weights)
    turn(1)
    up, down, pieces[1], pieces[7] = lax.optimization_barrier((up, down, pieces[1], pieces[7]))
    turn(2)

    parts = lax.all_to_all(x_sum(own, up, down), "z", 0, 0, tiled=True)
    parts, pieces[2], pieces[6] = lax.optimization_barrier((parts, pieces[2], pieces[6]))
    turn(3)
    returned = lax.all_to_all(z_sum(parts), ("y", "c"), 0, 0, tiled=True)
    returned, pieces[3], pieces[5] = lax.optimization_barrier((returned, pieces[3], pieces[5]))
    turn(4)
    combined, spread = combine(place, gate, grad, returned)
    gate_parts = lax.all_to_all(spread, ("x", "z"), 0, 0, tiled=True)
    hidden_grad, weight_grad, scale_grad = backward(where, *weights, [pieces[k] for k in range(NZ)])
    gate_parts, hidden_grad = lax.optimization_barrier((gate_parts, hidden_grad))
    gate_grad = gate_sum(gate_parts)
    return combined.T, gate_grad.T, hidden_grad[None], weight_grad[None], scale_grad.reshape(group_scales.shape)


def solution(mesh):
    fine = Mesh(mesh.devices.reshape(NY, NC, NX, NZ), ("y", "c", "x", "z"))
    expert, dp = ("y", "c"), ("x", "z")
    return jax.shard_map(
        on_device,
        mesh=fine,
        in_specs=(
            P(expert, dp, None),
            P(expert, dp, None),
            P(expert, dp, None),
            P(expert, None),
            P(expert, None),
            P(expert, dp),
        ),
        out_specs=(
            P(expert, dp),
            P(expert, None),
            P(expert, dp, None),
            P(expert, dp, None),
            P(expert, dp, None),
        ),
        check_vma=False,
    )
```

```python
import jax
import jax.numpy as jnp
from jax import lax
from jax.experimental import pallas as pl
from jax.experimental.pallas import tpu as pltpu
from jax.sharding import Mesh, PartitionSpec as P

EXPERTS = 8
GROUP = 32
CAP = 128
NY, NC, NX, NZ = 4, 2, 4, 8
COLS = 64
SLOTS = EXPERTS * CAP
BLOCK = NZ * COLS
SMALL = pltpu.CompilerParams(vmem_limit_bytes=16 * 1024 * 1024)
LARGE = pltpu.CompilerParams(vmem_limit_bytes=32 * 1024 * 1024)
F32, BF16, I32 = jnp.float32, jnp.bfloat16, jnp.int32


sds = jax.ShapeDtypeStruct
HBM, VMEM, SMEM = (pl.BlockSpec(memory_space=m) for m in (pltpu.HBM, pltpu.VMEM, pltpu.SMEM))


def near(array):
    return pltpu.with_memory_space_constraint(array, pltpu.VMEM)


def away(array):
    return pltpu.with_memory_space_constraint(array, pltpu.HBM)


def call(body, name, where, operands, outs, scratch=(), far=()):
    heads = [] if where is None else [where]
    return pl.pallas_call(
        body,
        in_specs=[SMEM] * len(heads) + [HBM] * len(far) + [VMEM] * len(operands),
        out_specs=[VMEM] * len(outs),
        out_shape=[pltpu.VMEM(shape, dtype) for shape, dtype in outs],
        scratch_shapes=list(scratch),
        compiler_params=SMALL,
        name=name,
    )(*heads, *[away(a) for a in far], *[near(a) for a in operands])


def dequant(codes_ref, scales_ref, tile, table_ref):
    units, width = codes_ref.shape
    tiles = scales_ref.shape[0] // (units // GROUP)
    for j in range(width // 128):
        lanes = slice(j * 128, (j + 1) * 128)
        for g in range(units // GROUP):
            rows = slice(g * GROUP, (g + 1) * GROUP)
            scale = scales_ref[pl.ds(g * tiles + tile + j, 1), :]
            table_ref[rows, lanes] = (codes_ref[rows, lanes].astype(F32) * scale).astype(BF16)


def picker(place_ref, k):
    slots = lax.broadcasted_iota(I32, (SLOTS, place_ref.shape[1]), 0)
    return (place_ref[k : k + 1, :] == slots).astype(BF16)


def slot_body(index_ref, gate_ref, grad_ref, place_ref, out_ref):
    tokens = index_ref.shape[1]
    experts = lax.broadcasted_iota(I32, (EXPERTS, tokens), 0)
    hot = [(index_ref[k : k + 1, :] == experts).astype(F32) for k in range(2)]
    row = lax.broadcasted_iota(I32, (tokens, tokens), 0)
    col = lax.broadcasted_iota(I32, (tokens, tokens), 1)
    before = (row < col).astype(BF16)
    counts = jnp.dot((hot[0] + hot[1]).astype(BF16), before, preferred_element_type=F32)
    for k in range(2):
        rank = jnp.sum(counts * hot[k], axis=0, keepdims=True).astype(I32)
        place_ref[k : k + 1, :] = jnp.where(rank < CAP, index_ref[k : k + 1, :] * CAP + rank, -1)
    grad = grad_ref[...].astype(F32)
    total = None
    for k in range(2):
        value = (gate_ref[k : k + 1, :] * grad).astype(BF16)
        piece = lax.dot_general(
            value, picker(place_ref, k), (((1,), (1,)), ((), ())), preferred_element_type=F32
        )
        total = piece if total is None else total + piece
    total = total.astype(BF16)
    for e in range(EXPERTS):
        for x in range(NX):
            out_ref[e * NX + x] = total[:, e * CAP : (e + 1) * CAP]


def slot_grads(index, gate, grad):
    outs = [(index.shape, I32), ((EXPERTS * NX, COLS, CAP), BF16)]
    return call(slot_body, "slot_grads", None, [index, gate, grad], outs)


def loads(where_ref, hops, hidden_hbm, codes_hbm, scales_hbm, hidden, codes, scales, sems):
    copies = [
        pltpu.make_async_copy(scales_hbm, scales, sems.at[0]),
        pltpu.make_async_copy(hidden_hbm, hidden, sems.at[1]),
    ]
    for i, hop in enumerate(hops):
        start = pl.multiple_of(lax.rem(where_ref[0] + hop, NX) * BLOCK, BLOCK)
        copies.append(pltpu.make_async_copy(codes_hbm.at[:, pl.ds(start, BLOCK)], codes.at[i], sems.at[2 + i]))
    for copy in copies:
        copy.start()
    copies[0].wait()
    return copies[1:]


def buffers(units, count):
    return [
        pltpu.VMEM((units, SLOTS), BF16),
        pltpu.VMEM((count, units, BLOCK), I32),
        pltpu.VMEM((units // GROUP * (NX * BLOCK // 128), 128), F32),
        pltpu.VMEM((units, BLOCK), BF16),
        pltpu.SemaphoreType.DMA((2 + count,)),
    ]


def block_value(where_ref, hops, hidden, codes, scales, table, copy, others=()):
    copy.wait()
    dequant(codes, scales, lax.rem(where_ref[0] + hops, NX) * (BLOCK // 128), table)
    for other in others:
        other.wait()
    return lax.dot_general(table[...], hidden[...], (((0,), (0,)), ((), ())), preferred_element_type=F32)


def far_body(where_ref, hidden_hbm, codes_hbm, scales_hbm, top_ref, bottom_ref, hidden, codes, scales, table, sems):
    first, *copies = loads(where_ref, (2,), hidden_hbm, codes_hbm, scales_hbm, hidden, codes, scales, sems)
    value = block_value(where_ref, 2, hidden, codes.at[0], scales, table, copies[0], (first,)).astype(BF16)
    top_ref[...] = value[: BLOCK // 2]
    bottom_ref[...] = value[BLOCK // 2 :]


def forward_far(where, *arrays):
    half = ((BLOCK // 2, SLOTS), BF16)
    return call(far_body, "forward_far", where, [], [half, half], buffers(arrays[0].shape[0], 1), arrays)


def join_body(
    where_ref, hidden_hbm, codes_hbm, scales_hbm, top_ref, bottom_ref, up_ref, down_ref, hidden, codes, scales, table, sems
):
    first, *copies = loads(where_ref, (1, 3), hidden_hbm, codes_hbm, scales_hbm, hidden, codes, scales, sems)
    half = BLOCK // 2
    value = block_value(where_ref, 1, hidden, codes.at[0], scales, table, copies[0], (first,))
    up_ref[:half] = (value[:half] + top_ref[...].astype(F32)).astype(BF16)
    up_ref[half:] = value[half:].astype(BF16)
    value = block_value(where_ref, 3, hidden, codes.at[1], scales, table, copies[1])
    down_ref[:half] = value[:half].astype(BF16)
    down_ref[half:] = (value[half:] + bottom_ref[...].astype(F32)).astype(BF16)


def forward_join(where, hidden, codes, scales, top, bottom):
    outs = [((BLOCK, SLOTS), BF16)] * 2
    far = (hidden, codes, scales)
    return call(join_body, "forward_join", where, [top, bottom], outs, buffers(hidden.shape[0], 2), far)


def own_body(where_ref, hidden_hbm, codes_hbm, scales_hbm, own_ref, hidden, codes, scales, table, sems):
    first, *copies = loads(where_ref, (0,), hidden_hbm, codes_hbm, scales_hbm, hidden, codes, scales, sems)
    own_ref[...] = block_value(where_ref, 0, hidden, codes.at[0], scales, table, copies[0], (first,))


def forward_own(where, *arrays):
    outs = [((BLOCK, SLOTS), F32)]
    return call(own_body, "forward_own", where, [], outs, buffers(arrays[0].shape[0], 1), arrays)[0]


def x_sum_body(where_ref, own_ref, up_ref, down_ref, ups_ref, downs_ref, far_ref, up2_ref, down2_ref, rest_ref):
    def total(hops):
        rows = pl.ds(pl.multiple_of(lax.rem(where_ref[1] + hops, NZ) * COLS, COLS), COLS)
        return own_ref[rows, :] + up_ref[rows, :].astype(F32) + down_ref[rows, :].astype(F32)

    ups_ref[0] = total(3).astype(BF16)
    ups_ref[1] = total(1).astype(BF16)
    downs_ref[0] = total(5).astype(BF16)
    downs_ref[1] = total(7).astype(BF16)
    far_ref[...] = total(4).astype(BF16)
    up2_ref[...] = total(2)
    down2_ref[...] = total(6)
    rest_ref[...] = total(0)


def x_sum(where, *arrays):
    one, two = (COLS, SLOTS), (2, COLS, SLOTS)
    outs = [(two, BF16), (two, BF16), (one, BF16), (one, F32), (one, F32), (one, F32)]
    return call(x_sum_body, "x_sum", where, arrays, outs)


def mid_sum_body(up2_ref, down2_ref, ups_ref, downs_ref, far_ref, up_out, down_out):
    up_out[...] = (up2_ref[...] + ups_ref[0].astype(F32) + far_ref[...].astype(F32)).astype(BF16)
    down_out[...] = (down2_ref[...] + downs_ref[0].astype(F32)).astype(BF16)


def mid_sum(*arrays):
    return call(mid_sum_body, "mid_sum", None, arrays, [((COLS, SLOTS), BF16)] * 2)


def z_sum_body(rest_ref, ups_ref, downs_ref, up_ref, down_ref, out_ref):
    total = rest_ref[...] + ups_ref[1].astype(F32) + downs_ref[1].astype(F32)
    total = (total + up_ref[...].astype(F32) + down_ref[...].astype(F32)).astype(BF16)
    for g in range(EXPERTS):
        out_ref[g] = total[:, g * CAP : (g + 1) * CAP]


def z_sum(*arrays):
    return call(z_sum_body, "z_sum", None, arrays, [((EXPERTS, COLS, CAP), BF16)])[0]


def combine_body(place_ref, gate_ref, grad_ref, back_ref, out_ref, spread_ref):
    back = jnp.concatenate([back_ref[e] for e in range(EXPERTS)], axis=1)
    grad = grad_ref[...].astype(F32)
    total = None
    for k in range(2):
        got = jnp.dot(back, picker(place_ref, k), preferred_element_type=F32)
        piece = gate_ref[k : k + 1, :] * got
        total = piece if total is None else total + piece
        part = jnp.sum(grad * got, axis=0, keepdims=True)
        for j in range(4):
            line = part[:, j * 128 : (j + 1) * 128]
            spread_ref[:, k * 4 + j : k * 4 + j + 1, :] = jnp.broadcast_to(line[None], (NX * NZ, 1, 128))
    out_ref[...] = total.astype(BF16)


def combine(place, gate, grad, back):
    outs = [(grad.shape, BF16), ((NX * NZ, 8, 128), F32)]
    return call(combine_body, "combine", None, [place, gate, grad, back], outs)


def gate_sum_body(parts_ref, out_ref):
    total = jnp.sum(parts_ref[...], axis=0)
    for k in range(2):
        for j in range(4):
            out_ref[k : k + 1, j * 128 : (j + 1) * 128] = total[k * 4 + j : k * 4 + j + 1, :]


def gate_sum(parts):
    return call(gate_sum_body, "gate_sum", None, [parts], [((2, 512), F32)])[0]


def backward_body(where_ref, hidden_hbm, codes_hbm, scales_hbm, *rest):
    pieces = rest[: NZ + 1]
    hidden_out, weight_out, scale_out = rest[NZ + 1 : NZ + 4]
    hidden, codes, scales, grads, table, weight, sems = rest[NZ + 4 :]
    units = hidden.shape[0]
    tiles = BLOCK // 128
    head = [
        pltpu.make_async_copy(hidden_hbm, hidden, sems.at[0]),
        pltpu.make_async_copy(scales_hbm, scales, sems.at[1]),
    ]
    parts, arrive = [], []
    for n in range(NX):
        lanes = slice(n * BLOCK, (n + 1) * BLOCK)
        parts.append(pltpu.make_async_copy(codes_hbm.at[:, lanes], codes.at[n], sems.at[2 + n]))
        arrive.append([])
        for k in range(NZ + 1):
            z = lax.rem(where_ref[1] + (k if k < NZ else 4), NZ)
            rows = pl.ds(pl.multiple_of(n * BLOCK + z * COLS, COLS), COLS)
            first = EXPERTS - pieces[k].shape[0] if k == NZ else 0
            groups = slice(first, first + pieces[k].shape[0])
            sem = sems.at[8 + n * (NZ + 1) + k]
            arrive[n].append(pltpu.make_async_copy(pieces[k].at[:, n], grads.at[groups, rows], sem))
    head[0].start()
    for copy in arrive[0]:
        copy.start()
    head[1].start()
    parts[0].start()
    for n in range(1, NX):
        for copy in arrive[n]:
            copy.start()
        parts[n].start()
    head[0].wait()
    head[1].wait()
    copies = []
    for n in range(NX):
        lanes = slice(n * BLOCK, (n + 1) * BLOCK)
        for copy in arrive[n]:
            copy.wait()
        block = jnp.concatenate([grads[g, lanes, :] for g in range(EXPERTS)], axis=1)
        slot = n % 2
        if n >= 2:
            copies[n - 2].wait()
        weight[slot] = lax.dot_general(
            hidden[...], block, (((1,), (1,)), ((), ())), preferred_element_type=F32
        )
        copies.append(pltpu.make_async_copy(weight.at[slot], weight_out.at[:, lanes], sems.at[6 + slot]))
        copies[n].start()
        parts[n].wait()
        dequant(codes.at[n], scales, n * tiles, table.at[:, lanes])
        for g in range(units // GROUP):
            rows = slice(g * GROUP, (g + 1) * GROUP)
            line = jnp.sum(weight[slot, rows, :] * codes[n, rows, :].astype(F32), axis=0, keepdims=True)
            for j in range(tiles):
                row = (g * NX + n) * tiles + j
                scale_out[row : row + 1, :] = line[:, j * 128 : (j + 1) * 128]
    block = jnp.concatenate([grads[g] for g in range(EXPERTS)], axis=1)
    hidden_out[...] = jnp.dot(table[...], block, preferred_element_type=F32).astype(BF16)
    copies[2].wait()
    copies[3].wait()


def backward(where, hidden, codes, scales, pieces):
    units, slots = hidden.shape
    features = codes.shape[1]
    pieces = [a.reshape(-1, NX, COLS, CAP) for a in pieces]
    return pl.pallas_call(
        backward_body,
        in_specs=[SMEM] + [HBM] * (4 + NZ),
        out_specs=[VMEM, HBM, VMEM],
        out_shape=[sds((units, slots), BF16), sds((units, features), F32), sds(scales.shape, F32)],
        scratch_shapes=[
            pltpu.VMEM((units, slots), BF16),
            pltpu.VMEM((NX, units, BLOCK), I32),
            pltpu.VMEM(scales.shape, F32),
            pltpu.VMEM((EXPERTS, features, CAP), BF16),
            pltpu.VMEM((units, features), BF16),
            pltpu.VMEM((2, units, BLOCK), F32),
            pltpu.SemaphoreType.DMA((8 + NX * (NZ + 1),)),
        ],
        compiler_params=LARGE,
        name="backward",
    )(where, *[away(a) for a in (hidden, codes, scales, *pieces)])


def shift(value, axis, by):
    size = NX if axis == "x" else NZ
    return lax.ppermute(value, axis, [(i, (i + by) % size) for i in range(size)])


def on_device(hidden, weight_codes, group_scales, expert_index, gate_values, output_grad):
    weights = (hidden[0], weight_codes[0], group_scales.reshape(-1, 128))
    index, gate, grad = expert_index.T, gate_values.T, output_grad.T
    where = jnp.stack([lax.axis_index("x"), lax.axis_index("z")]).astype(I32)

    far_top, far_bottom = forward_far(where, *weights)
    far_top = shift(far_top, "x", 1)
    far_bottom = shift(far_bottom, "x", -1)

    place, outbound = slot_grads(index, gate, grad)
    pieces = {0: lax.all_to_all(outbound, ("y", "c", "x"), 0, 0, tiled=True)}

    def turn(hop):
        pieces[hop] = shift(pieces[hop - 1], "z", -1)
        pieces[NZ - hop] = shift(pieces[(NZ - hop + 1) % NZ], "z", 1)

    far_top, far_bottom, pieces[0] = lax.optimization_barrier((far_top, far_bottom, pieces[0]))
    up, down = forward_join(where, *weights, far_top, far_bottom)
    where_late, up, down = lax.optimization_barrier((where, up, down))
    up = shift(up, "x", 1)
    down = shift(down, "x", -1)
    own = forward_own(where_late, *weights)
    turn(1)
    turn(2)
    up, down, pieces[2], pieces[6] = lax.optimization_barrier((up, down, pieces[2], pieces[6]))

    ups, downs, far, up2, down2, rest = x_sum(where, own, up, down)
    ups, downs, far = shift(ups, "z", 1), shift(downs, "z", -1), shift(far, "z", 2)
    up2, down2 = mid_sum(up2, down2, ups, downs, far)
    up2, pieces[2], pieces[6] = lax.optimization_barrier((up2, pieces[2], pieces[6]))
    turn(3)
    summed = z_sum(rest, ups, downs, shift(up2, "z", 2), shift(down2, "z", -2))
    returned = lax.all_to_all(summed, ("y", "c"), 0, 0, tiled=True)
    returned, pieces[3], pieces[5] = lax.optimization_barrier((returned, pieces[3], pieces[5]))
    last = [shift(pieces[3][: EXPERTS * NX // 2], "z", -1), shift(pieces[5][EXPERTS * NX // 2 :], "z", 1)]
    combined, spread = combine(place, gate, grad, returned)
    gate_parts = lax.all_to_all(spread, ("x", "z"), 0, 0, tiled=True)
    ordered = [pieces[k] if k != 4 else last[0] for k in range(NZ)] + [last[1]]
    hidden_grad, weight_grad, scale_grad = backward(where, *weights, ordered)
    gate_parts, hidden_grad = lax.optimization_barrier((gate_parts, hidden_grad))
    gate_grad = gate_sum(gate_parts)
    return combined.T, gate_grad.T, hidden_grad[None], weight_grad[None], scale_grad.reshape(group_scales.shape)


def solution(mesh):
    fine = Mesh(mesh.devices.reshape(NY, NC, NX, NZ), ("y", "c", "x", "z"))
    expert, dp = ("y", "c"), ("x", "z")
    return jax.shard_map(
        on_device,
        mesh=fine,
        in_specs=(
            P(expert, dp, None),
            P(expert, dp, None),
            P(expert, dp, None),
            P(expert, None),
            P(expert, None),
            P(expert, dp),
        ),
        out_specs=(
            P(expert, dp),
            P(expert, None),
            P(expert, dp, None),
            P(expert, dp, None),
            P(expert, dp, None),
        ),
        check_vma=False,
    )
```

```python
import jax
import jax.numpy as jnp
from jax import lax
from jax.experimental import pallas as pl
from jax.experimental.pallas import tpu as pltpu
from jax.sharding import Mesh, PartitionSpec as P

EXPERTS = 8
GROUP = 32
CAP = 128
NY, NC, NX, NZ = 4, 2, 4, 8
COLS = 64
SLOTS = EXPERTS * CAP
BLOCK = NZ * COLS
SMALL = pltpu.CompilerParams(vmem_limit_bytes=16 * 1024 * 1024)
LARGE = pltpu.CompilerParams(vmem_limit_bytes=32 * 1024 * 1024)
F32, BF16, I32 = jnp.float32, jnp.bfloat16, jnp.int32


sds = jax.ShapeDtypeStruct
HBM, VMEM, SMEM = (pl.BlockSpec(memory_space=m) for m in (pltpu.HBM, pltpu.VMEM, pltpu.SMEM))


def near(array):
    return pltpu.with_memory_space_constraint(array, pltpu.VMEM)


def away(array):
    return pltpu.with_memory_space_constraint(array, pltpu.HBM)


def call(body, name, where, operands, outs, scratch=(), far=()):
    heads = [] if where is None else [where]
    return pl.pallas_call(
        body,
        in_specs=[SMEM] * len(heads) + [HBM] * len(far) + [VMEM] * len(operands),
        out_specs=[VMEM] * len(outs),
        out_shape=[pltpu.VMEM(shape, dtype) for shape, dtype in outs],
        scratch_shapes=list(scratch),
        compiler_params=SMALL,
        name=name,
    )(*heads, *[away(a) for a in far], *[near(a) for a in operands])


def dequant(codes_ref, scales_ref, tile, table_ref):
    units, width = codes_ref.shape
    tiles = scales_ref.shape[0] // (units // GROUP)
    for j in range(width // 128):
        lanes = slice(j * 128, (j + 1) * 128)
        for g in range(units // GROUP):
            rows = slice(g * GROUP, (g + 1) * GROUP)
            scale = scales_ref[pl.ds(g * tiles + tile + j, 1), :]
            table_ref[rows, lanes] = (codes_ref[rows, lanes].astype(F32) * scale).astype(BF16)


def picker(place_ref, k):
    slots = lax.broadcasted_iota(I32, (SLOTS, place_ref.shape[1]), 0)
    return (place_ref[k : k + 1, :] == slots).astype(BF16)


def slot_body(index_ref, gate_ref, grad_ref, place_ref, out_ref):
    tokens = index_ref.shape[1]
    experts = lax.broadcasted_iota(I32, (EXPERTS, tokens), 0)
    hot = [(index_ref[k : k + 1, :] == experts).astype(F32) for k in range(2)]
    row = lax.broadcasted_iota(I32, (tokens, tokens), 0)
    col = lax.broadcasted_iota(I32, (tokens, tokens), 1)
    before = (row < col).astype(BF16)
    counts = jnp.dot((hot[0] + hot[1]).astype(BF16), before, preferred_element_type=F32)
    for k in range(2):
        rank = jnp.sum(counts * hot[k], axis=0, keepdims=True).astype(I32)
        place_ref[k : k + 1, :] = jnp.where(rank < CAP, index_ref[k : k + 1, :] * CAP + rank, -1)
    grad = grad_ref[...].astype(F32)
    total = None
    for k in range(2):
        value = (gate_ref[k : k + 1, :] * grad).astype(BF16)
        piece = lax.dot_general(
            value, picker(place_ref, k), (((1,), (1,)), ((), ())), preferred_element_type=F32
        )
        total = piece if total is None else total + piece
    total = total.astype(BF16)
    for e in range(EXPERTS):
        for x in range(NX):
            out_ref[e * NX + x] = total[:, e * CAP : (e + 1) * CAP]


def slot_grads(index, gate, grad):
    outs = [(index.shape, I32), ((EXPERTS * NX, COLS, CAP), BF16)]
    return call(slot_body, "slot_grads", None, [index, gate, grad], outs)


def loads(where_ref, hops, hidden_hbm, codes_hbm, scales_hbm, hidden, codes, scales, sems):
    copies = [
        pltpu.make_async_copy(scales_hbm, scales, sems.at[0]),
        pltpu.make_async_copy(hidden_hbm, hidden, sems.at[1]),
    ]
    for i, hop in enumerate(hops):
        start = pl.multiple_of(lax.rem(where_ref[0] + hop, NX) * BLOCK, BLOCK)
        copies.append(pltpu.make_async_copy(codes_hbm.at[:, pl.ds(start, BLOCK)], codes.at[i], sems.at[2 + i]))
    for copy in copies:
        copy.start()
    copies[0].wait()
    return copies[1:]


def buffers(units, count):
    return [
        pltpu.VMEM((units, SLOTS), BF16),
        pltpu.VMEM((count, units, BLOCK), I32),
        pltpu.VMEM((units // GROUP * (NX * BLOCK // 128), 128), F32),
        pltpu.VMEM((units, BLOCK), BF16),
        pltpu.SemaphoreType.DMA((2 + count,)),
    ]


def block_value(where_ref, hops, hidden, codes, scales, table, copy, others=()):
    copy.wait()
    dequant(codes, scales, lax.rem(where_ref[0] + hops, NX) * (BLOCK // 128), table)
    for other in others:
        other.wait()
    return lax.dot_general(table[...], hidden[...], (((0,), (0,)), ((), ())), preferred_element_type=F32)


def far_body(where_ref, hidden_hbm, codes_hbm, scales_hbm, top_ref, bottom_ref, hidden, codes, scales, table, sems):
    first, *copies = loads(where_ref, (2,), hidden_hbm, codes_hbm, scales_hbm, hidden, codes, scales, sems)
    value = block_value(where_ref, 2, hidden, codes.at[0], scales, table, copies[0], (first,)).astype(BF16)
    top_ref[...] = value[: BLOCK // 2]
    bottom_ref[...] = value[BLOCK // 2 :]


def forward_far(where, *arrays):
    half = ((BLOCK // 2, SLOTS), BF16)
    return call(far_body, "forward_far", where, [], [half, half], buffers(arrays[0].shape[0], 1), arrays)


def join_body(
    where_ref, hidden_hbm, codes_hbm, scales_hbm, top_ref, bottom_ref, up_ref, down_ref, hidden, codes, scales, table, sems
):
    first, *copies = loads(where_ref, (1, 3), hidden_hbm, codes_hbm, scales_hbm, hidden, codes, scales, sems)
    half = BLOCK // 2
    value = block_value(where_ref, 1, hidden, codes.at[0], scales, table, copies[0], (first,))
    up_ref[:half] = (value[:half] + top_ref[...].astype(F32)).astype(BF16)
    up_ref[half:] = value[half:].astype(BF16)
    value = block_value(where_ref, 3, hidden, codes.at[1], scales, table, copies[1])
    down_ref[:half] = value[:half].astype(BF16)
    down_ref[half:] = (value[half:] + bottom_ref[...].astype(F32)).astype(BF16)


def forward_join(where, hidden, codes, scales, top, bottom):
    outs = [((BLOCK, SLOTS), BF16)] * 2
    far = (hidden, codes, scales)
    return call(join_body, "forward_join", where, [top, bottom], outs, buffers(hidden.shape[0], 2), far)


def own_body(where_ref, hidden_hbm, codes_hbm, scales_hbm, own_ref, hidden, codes, scales, table, sems):
    first, *copies = loads(where_ref, (0,), hidden_hbm, codes_hbm, scales_hbm, hidden, codes, scales, sems)
    own_ref[...] = block_value(where_ref, 0, hidden, codes.at[0], scales, table, copies[0], (first,))


def forward_own(where, *arrays):
    outs = [((BLOCK, SLOTS), F32)]
    return call(own_body, "forward_own", where, [], outs, buffers(arrays[0].shape[0], 1), arrays)[0]


def x_sum_body(where_ref, own_ref, up_ref, down_ref, ups_ref, downs_ref, far_ref, up2_ref, down2_ref, rest_ref):
    def total(hops):
        rows = pl.ds(pl.multiple_of(lax.rem(where_ref[1] + hops, NZ) * COLS, COLS), COLS)
        return own_ref[rows, :] + up_ref[rows, :].astype(F32) + down_ref[rows, :].astype(F32)

    ups_ref[0] = total(3).astype(BF16)
    ups_ref[1] = total(1).astype(BF16)
    downs_ref[0] = total(5).astype(BF16)
    downs_ref[1] = total(7).astype(BF16)
    far_ref[...] = total(4).astype(BF16)
    up2_ref[...] = total(2)
    down2_ref[...] = total(6)
    rest_ref[...] = total(0)


def x_sum(where, *arrays):
    one, two = (COLS, SLOTS), (2, COLS, SLOTS)
    outs = [(two, BF16), (two, BF16), (one, BF16), (one, F32), (one, F32), (one, F32)]
    return call(x_sum_body, "x_sum", where, arrays, outs)


def mid_sum_body(up2_ref, down2_ref, ups_ref, downs_ref, far_ref, up_out, down_out):
    up_out[...] = (up2_ref[...] + ups_ref[0].astype(F32) + far_ref[...].astype(F32)).astype(BF16)
    down_out[...] = (down2_ref[...] + downs_ref[0].astype(F32)).astype(BF16)


def mid_sum(*arrays):
    return call(mid_sum_body, "mid_sum", None, arrays, [((COLS, SLOTS), BF16)] * 2)


def z_sum_body(rest_ref, ups_ref, downs_ref, up_ref, down_ref, out_ref):
    total = rest_ref[...] + ups_ref[1].astype(F32) + downs_ref[1].astype(F32)
    total = (total + up_ref[...].astype(F32) + down_ref[...].astype(F32)).astype(BF16)
    for g in range(EXPERTS):
        out_ref[g] = total[:, g * CAP : (g + 1) * CAP]


def z_sum(*arrays):
    return call(z_sum_body, "z_sum", None, arrays, [((EXPERTS, COLS, CAP), BF16)])[0]


def combine_body(place_ref, gate_ref, grad_ref, back_ref, out_ref, spread_ref):
    back = jnp.concatenate([back_ref[e] for e in range(EXPERTS)], axis=1)
    grad = grad_ref[...].astype(F32)
    total = None
    for k in range(2):
        got = jnp.dot(back, picker(place_ref, k), preferred_element_type=F32)
        piece = gate_ref[k : k + 1, :] * got
        total = piece if total is None else total + piece
        part = jnp.sum(grad * got, axis=0, keepdims=True)
        for j in range(4):
            line = part[:, j * 128 : (j + 1) * 128]
            spread_ref[:, k * 4 + j : k * 4 + j + 1, :] = jnp.broadcast_to(line[None], (NX * NZ, 1, 128))
    out_ref[...] = total.astype(BF16)


def combine(place, gate, grad, back):
    outs = [(grad.shape, BF16), ((NX * NZ, 8, 128), F32)]
    return call(combine_body, "combine", None, [place, gate, grad, back], outs)


def gate_sum_body(parts_ref, out_ref):
    total = jnp.sum(parts_ref[...], axis=0)
    for k in range(2):
        for j in range(4):
            out_ref[k : k + 1, j * 128 : (j + 1) * 128] = total[k * 4 + j : k * 4 + j + 1, :]


def gate_sum(parts):
    return call(gate_sum_body, "gate_sum", None, [parts], [((2, 512), F32)])[0]


def backward_body(where_ref, hidden_hbm, codes_hbm, scales_hbm, *rest):
    pieces = rest[: NZ + 1]
    hidden_out, weight_out, scale_out = rest[NZ + 1 : NZ + 4]
    hidden, codes, scales, grads, table, weight, sems = rest[NZ + 4 :]
    units = hidden.shape[0]
    tiles = BLOCK // 128
    head = [
        pltpu.make_async_copy(hidden_hbm, hidden, sems.at[0]),
        pltpu.make_async_copy(scales_hbm, scales, sems.at[1]),
    ]
    parts, arrive = [], []
    for n in range(NX):
        lanes = slice(n * BLOCK, (n + 1) * BLOCK)
        parts.append(pltpu.make_async_copy(codes_hbm.at[:, lanes], codes.at[n], sems.at[2 + n]))
        arrive.append([])
        for k in range(NZ + 1):
            z = lax.rem(where_ref[1] + (k if k < NZ else 4), NZ)
            rows = pl.ds(pl.multiple_of(n * BLOCK + z * COLS, COLS), COLS)
            first = EXPERTS - pieces[k].shape[0] if k == NZ else 0
            groups = slice(first, first + pieces[k].shape[0])
            sem = sems.at[8 + n * (NZ + 1) + k]
            arrive[n].append(pltpu.make_async_copy(pieces[k].at[:, n], grads.at[groups, rows], sem))
    head[0].start()
    for copy in arrive[0]:
        copy.start()
    head[1].start()
    parts[0].start()
    for n in range(1, NX):
        for copy in arrive[n]:
            copy.start()
        parts[n].start()
    head[0].wait()
    head[1].wait()
    copies = []
    for n in range(NX):
        lanes = slice(n * BLOCK, (n + 1) * BLOCK)
        for copy in arrive[n]:
            copy.wait()
        block = jnp.concatenate([grads[g, lanes, :] for g in range(EXPERTS)], axis=1)
        slot = n % 2
        if n >= 2:
            copies[n - 2].wait()
        weight[slot] = lax.dot_general(
            hidden[...], block, (((1,), (1,)), ((), ())), preferred_element_type=F32
        )
        copies.append(pltpu.make_async_copy(weight.at[slot], weight_out.at[:, lanes], sems.at[6 + slot]))
        copies[n].start()
        parts[n].wait()
        dequant(codes.at[n], scales, n * tiles, table.at[:, lanes])
        for g in range(units // GROUP):
            rows = slice(g * GROUP, (g + 1) * GROUP)
            line = jnp.sum(weight[slot, rows, :] * codes[n, rows, :].astype(F32), axis=0, keepdims=True)
            for j in range(tiles):
                row = (g * NX + n) * tiles + j
                scale_out[row : row + 1, :] = line[:, j * 128 : (j + 1) * 128]
    block = jnp.concatenate([grads[g] for g in range(EXPERTS)], axis=1)
    hidden_out[...] = jnp.dot(table[...], block, preferred_element_type=F32).astype(BF16)
    copies[2].wait()
    copies[3].wait()


def backward(where, hidden, codes, scales, pieces):
    units, slots = hidden.shape
    features = codes.shape[1]
    pieces = [a.reshape(-1, NX, COLS, CAP) for a in pieces]
    return pl.pallas_call(
        backward_body,
        in_specs=[SMEM] + [HBM] * (4 + NZ),
        out_specs=[VMEM, HBM, VMEM],
        out_shape=[sds((units, slots), BF16), sds((units, features), F32), sds(scales.shape, F32)],
        scratch_shapes=[
            pltpu.VMEM((units, slots), BF16),
            pltpu.VMEM((NX, units, BLOCK), I32),
            pltpu.VMEM(scales.shape, F32),
            pltpu.VMEM((EXPERTS, features, CAP), BF16),
            pltpu.VMEM((units, features), BF16),
            pltpu.VMEM((2, units, BLOCK), F32),
            pltpu.SemaphoreType.DMA((8 + NX * (NZ + 1),)),
        ],
        compiler_params=LARGE,
        name="backward",
    )(where, *[away(a) for a in (hidden, codes, scales, *pieces)])


def shift(value, axis, by):
    size = NX if axis == "x" else NZ
    return lax.ppermute(value, axis, [(i, (i + by) % size) for i in range(size)])


def on_device(hidden, weight_codes, group_scales, expert_index, gate_values, output_grad):
    weights = (hidden[0], weight_codes[0], group_scales.reshape(-1, 128))
    index, gate, grad = expert_index.T, gate_values.T, output_grad.T
    where = jnp.stack([lax.axis_index("x"), lax.axis_index("z")]).astype(I32)

    far_top, far_bottom = forward_far(where, *weights)
    where_late, index, far_top, far_bottom = lax.optimization_barrier((where, index, far_top, far_bottom))
    far_top = shift(far_top, "x", 1)
    far_bottom = shift(far_bottom, "x", -1)
    own = forward_own(where_late, *weights)
    place, outbound = slot_grads(index, gate, grad)
    far_top, far_bottom, own, outbound = lax.optimization_barrier((far_top, far_bottom, own, outbound))
    up, down = forward_join(where, *weights, far_top, far_bottom)
    up, down, outbound = lax.optimization_barrier((up, down, outbound))
    up = shift(up, "x", 1)
    down = shift(down, "x", -1)

    pieces = {0: lax.all_to_all(outbound, ("y", "c", "x"), 0, 0, tiled=True)}

    def turn(hop):
        pieces[hop] = shift(pieces[hop - 1], "z", -1)
        pieces[NZ - hop] = shift(pieces[(NZ - hop + 1) % NZ], "z", 1)

    turn(1)
    up, down, _ = lax.optimization_barrier((up, down, pieces[0]))

    ups, downs, far, up2, down2, rest = x_sum(where, own, up, down)
    ups, downs, far = shift(ups, "z", 1), shift(downs, "z", -1), shift(far, "z", 2)
    up2, down2 = mid_sum(up2, down2, ups, downs, far)
    up2, down2, pieces[1], pieces[7] = lax.optimization_barrier((up2, down2, pieces[1], pieces[7]))
    turn(2)
    up2, down2 = shift(up2, "z", 2), shift(down2, "z", -2)
    up2, down2, pieces[2], pieces[6] = lax.optimization_barrier((up2, down2, pieces[2], pieces[6]))
    turn(3)
    returned = lax.all_to_all(z_sum(rest, ups, downs, up2, down2), ("y", "c"), 0, 0, tiled=True)
    last = [shift(pieces[3][: EXPERTS * NX // 2], "z", -1), shift(pieces[5][EXPERTS * NX // 2 :], "z", 1)]
    combined, spread = combine(place, gate, grad, returned)
    gate_parts = lax.all_to_all(spread, ("x", "z"), 0, 0, tiled=True)
    ordered = [pieces[k] if k != 4 else last[0] for k in range(NZ)] + [last[1]]
    hidden_grad, weight_grad, scale_grad = backward(where, *weights, ordered)
    gate_parts, hidden_grad = lax.optimization_barrier((gate_parts, hidden_grad))
    gate_grad = gate_sum(gate_parts)
    return combined.T, gate_grad.T, hidden_grad[None], weight_grad[None], scale_grad.reshape(group_scales.shape)


def solution(mesh):
    fine = Mesh(mesh.devices.reshape(NY, NC, NX, NZ), ("y", "c", "x", "z"))
    expert, dp = ("y", "c"), ("x", "z")
    return jax.shard_map(
        on_device,
        mesh=fine,
        in_specs=(
            P(expert, dp, None),
            P(expert, dp, None),
            P(expert, dp, None),
            P(expert, None),
            P(expert, None),
            P(expert, dp),
        ),
        out_specs=(
            P(expert, dp),
            P(expert, None),
            P(expert, dp, None),
            P(expert, dp, None),
            P(expert, dp, None),
        ),
        check_vma=False,
    )
```

```python
import jax
import jax.numpy as jnp
from jax import lax
from jax.experimental import pallas as pl
from jax.experimental.pallas import tpu as pltpu
from jax.sharding import Mesh, PartitionSpec as P

EXPERTS = 8
GROUP = 32
CAP = 128
NY, NC, NX, NZ = 4, 2, 4, 8
COLS = 64
SLOTS = EXPERTS * CAP
BLOCK = NZ * COLS
SMALL = pltpu.CompilerParams(vmem_limit_bytes=16 * 1024 * 1024)
LARGE = pltpu.CompilerParams(vmem_limit_bytes=32 * 1024 * 1024)
F32, BF16, I32 = jnp.float32, jnp.bfloat16, jnp.int32


sds = jax.ShapeDtypeStruct
HBM, VMEM, SMEM = (pl.BlockSpec(memory_space=m) for m in (pltpu.HBM, pltpu.VMEM, pltpu.SMEM))


def near(array):
    return pltpu.with_memory_space_constraint(array, pltpu.VMEM)


def away(array):
    return pltpu.with_memory_space_constraint(array, pltpu.HBM)


def call(body, name, where, operands, outs, scratch=(), far=()):
    heads = [] if where is None else [where]
    return pl.pallas_call(
        body,
        in_specs=[SMEM] * len(heads) + [HBM] * len(far) + [VMEM] * len(operands),
        out_specs=[VMEM] * len(outs),
        out_shape=[pltpu.VMEM(shape, dtype) for shape, dtype in outs],
        scratch_shapes=list(scratch),
        compiler_params=SMALL,
        name=name,
    )(*heads, *[away(a) for a in far], *[near(a) for a in operands])


def dequant(codes_ref, scales_ref, tile, table_ref):
    units, width = codes_ref.shape
    tiles = scales_ref.shape[0] // (units // GROUP)
    for j in range(width // 128):
        lanes = slice(j * 128, (j + 1) * 128)
        for g in range(units // GROUP):
            rows = slice(g * GROUP, (g + 1) * GROUP)
            scale = scales_ref[pl.ds(g * tiles + tile + j, 1), :]
            table_ref[rows, lanes] = (codes_ref[rows, lanes].astype(F32) * scale).astype(BF16)


def picker(place_ref, k):
    slots = lax.broadcasted_iota(I32, (SLOTS, place_ref.shape[1]), 0)
    return (place_ref[k : k + 1, :] == slots).astype(BF16)


def slot_body(index_ref, gate_ref, grad_ref, place_ref, out_ref):
    tokens = index_ref.shape[1]
    experts = lax.broadcasted_iota(I32, (EXPERTS, tokens), 0)
    hot = [(index_ref[k : k + 1, :] == experts).astype(F32) for k in range(2)]
    row = lax.broadcasted_iota(I32, (tokens, tokens), 0)
    col = lax.broadcasted_iota(I32, (tokens, tokens), 1)
    before = (row < col).astype(BF16)
    counts = jnp.dot((hot[0] + hot[1]).astype(BF16), before, preferred_element_type=F32)
    for k in range(2):
        rank = jnp.sum(counts * hot[k], axis=0, keepdims=True).astype(I32)
        place_ref[k : k + 1, :] = jnp.where(rank < CAP, index_ref[k : k + 1, :] * CAP + rank, -1)
    grad = grad_ref[...].astype(F32)
    total = None
    for k in range(2):
        value = (gate_ref[k : k + 1, :] * grad).astype(BF16)
        piece = lax.dot_general(
            value, picker(place_ref, k), (((1,), (1,)), ((), ())), preferred_element_type=F32
        )
        total = piece if total is None else total + piece
    total = total.astype(BF16)
    for e in range(EXPERTS):
        out_ref[e] = total[:, e * CAP : (e + 1) * CAP]


def slot_grads(index, gate, grad):
    outs = [(index.shape, I32), ((EXPERTS, COLS, CAP), BF16)]
    return call(slot_body, "slot_grads", None, [index, gate, grad], outs)


def loads(where_ref, hops, hidden_hbm, codes_hbm, scales_hbm, hidden, codes, scales, sems):
    copies = [
        pltpu.make_async_copy(scales_hbm, scales, sems.at[0]),
        pltpu.make_async_copy(hidden_hbm, hidden, sems.at[1]),
    ]
    for i, hop in enumerate(hops):
        start = pl.multiple_of(lax.rem(where_ref[0] + hop, NX) * BLOCK, BLOCK)
        copies.append(pltpu.make_async_copy(codes_hbm.at[:, pl.ds(start, BLOCK)], codes.at[i], sems.at[2 + i]))
    for copy in copies:
        copy.start()
    copies[0].wait()
    return copies[1:]


def buffers(units, count):
    return [
        pltpu.VMEM((units, SLOTS), BF16),
        pltpu.VMEM((count, units, BLOCK), I32),
        pltpu.VMEM((units // GROUP * (NX * BLOCK // 128), 128), F32),
        pltpu.VMEM((units, BLOCK), BF16),
        pltpu.SemaphoreType.DMA((2 + count,)),
    ]


def block_value(where_ref, hops, hidden, codes, scales, table, copy, others=()):
    copy.wait()
    dequant(codes, scales, lax.rem(where_ref[0] + hops, NX) * (BLOCK // 128), table)
    for other in others:
        other.wait()
    return lax.dot_general(table[...], hidden[...], (((0,), (0,)), ((), ())), preferred_element_type=F32)


def far_body(where_ref, hidden_hbm, codes_hbm, scales_hbm, top_ref, bottom_ref, hidden, codes, scales, table, sems):
    first, *copies = loads(where_ref, (2,), hidden_hbm, codes_hbm, scales_hbm, hidden, codes, scales, sems)
    value = block_value(where_ref, 2, hidden, codes.at[0], scales, table, copies[0], (first,)).astype(BF16)
    top_ref[...] = value[: BLOCK // 2]
    bottom_ref[...] = value[BLOCK // 2 :]


def forward_far(where, *arrays):
    half = ((BLOCK // 2, SLOTS), BF16)
    return call(far_body, "forward_far", where, [], [half, half], buffers(arrays[0].shape[0], 1), arrays)


def join_body(
    where_ref, hidden_hbm, codes_hbm, scales_hbm, top_ref, bottom_ref, up_ref, down_ref, hidden, codes, scales, table, sems
):
    first, *copies = loads(where_ref, (1, 3), hidden_hbm, codes_hbm, scales_hbm, hidden, codes, scales, sems)
    half = BLOCK // 2
    value = block_value(where_ref, 1, hidden, codes.at[0], scales, table, copies[0], (first,))
    up_ref[:half] = (value[:half] + top_ref[...].astype(F32)).astype(BF16)
    up_ref[half:] = value[half:].astype(BF16)
    value = block_value(where_ref, 3, hidden, codes.at[1], scales, table, copies[1])
    down_ref[:half] = value[:half].astype(BF16)
    down_ref[half:] = (value[half:] + bottom_ref[...].astype(F32)).astype(BF16)


def forward_join(where, hidden, codes, scales, top, bottom):
    outs = [((BLOCK, SLOTS), BF16)] * 2
    far = (hidden, codes, scales)
    return call(join_body, "forward_join", where, [top, bottom], outs, buffers(hidden.shape[0], 2), far)


def own_body(where_ref, hidden_hbm, codes_hbm, scales_hbm, own_ref, hidden, codes, scales, table, sems):
    first, *copies = loads(where_ref, (0,), hidden_hbm, codes_hbm, scales_hbm, hidden, codes, scales, sems)
    own_ref[...] = block_value(where_ref, 0, hidden, codes.at[0], scales, table, copies[0], (first,))


def forward_own(where, *arrays):
    outs = [((BLOCK, SLOTS), F32)]
    return call(own_body, "forward_own", where, [], outs, buffers(arrays[0].shape[0], 1), arrays)[0]


def x_sum_body(where_ref, own_ref, up_ref, down_ref, ups_ref, downs_ref, far_ref, up2_ref, down2_ref, rest_ref):
    def total(hops):
        rows = pl.ds(pl.multiple_of(lax.rem(where_ref[1] + hops, NZ) * COLS, COLS), COLS)
        return own_ref[rows, :] + up_ref[rows, :].astype(F32) + down_ref[rows, :].astype(F32)

    ups_ref[0] = total(3).astype(BF16)
    ups_ref[1] = total(1).astype(BF16)
    downs_ref[0] = total(5).astype(BF16)
    downs_ref[1] = total(7).astype(BF16)
    far_ref[...] = total(4).astype(BF16)
    up2_ref[...] = total(2)
    down2_ref[...] = total(6)
    rest_ref[...] = total(0)


def x_sum(where, *arrays):
    one, two = (COLS, SLOTS), (2, COLS, SLOTS)
    outs = [(two, BF16), (two, BF16), (one, BF16), (one, F32), (one, F32), (one, F32)]
    return call(x_sum_body, "x_sum", where, arrays, outs)


def mid_sum_body(up2_ref, down2_ref, ups_ref, downs_ref, far_ref, up_out, down_out):
    up_out[...] = (up2_ref[...] + ups_ref[0].astype(F32) + far_ref[...].astype(F32)).astype(BF16)
    down_out[...] = (down2_ref[...] + downs_ref[0].astype(F32)).astype(BF16)


def mid_sum(*arrays):
    return call(mid_sum_body, "mid_sum", None, arrays, [((COLS, SLOTS), BF16)] * 2)


def z_sum_body(rest_ref, ups_ref, downs_ref, up_ref, down_ref, out_ref):
    total = rest_ref[...] + ups_ref[1].astype(F32) + downs_ref[1].astype(F32)
    total = (total + up_ref[...].astype(F32) + down_ref[...].astype(F32)).astype(BF16)
    for g in range(EXPERTS):
        out_ref[g] = total[:, g * CAP : (g + 1) * CAP]


def z_sum(*arrays):
    return call(z_sum_body, "z_sum", None, arrays, [((EXPERTS, COLS, CAP), BF16)])[0]


def combine_body(place_ref, gate_ref, grad_ref, back_ref, out_ref, spread_ref):
    back = jnp.concatenate([back_ref[e] for e in range(EXPERTS)], axis=1)
    grad = grad_ref[...].astype(F32)
    total = None
    for k in range(2):
        got = jnp.dot(back, picker(place_ref, k), preferred_element_type=F32)
        piece = gate_ref[k : k + 1, :] * got
        total = piece if total is None else total + piece
        part = jnp.sum(grad * got, axis=0, keepdims=True)
        for j in range(4):
            line = part[:, j * 128 : (j + 1) * 128]
            spread_ref[:, k * 4 + j : k * 4 + j + 1, :] = jnp.broadcast_to(line[None], (NX * NZ, 1, 128))
    out_ref[...] = total.astype(BF16)


def combine(place, gate, grad, back):
    outs = [(grad.shape, BF16), ((NX * NZ, 8, 128), F32)]
    return call(combine_body, "combine", None, [place, gate, grad, back], outs)


def gate_sum_body(parts_ref, out_ref):
    total = jnp.sum(parts_ref[...], axis=0)
    for k in range(2):
        for j in range(4):
            out_ref[k : k + 1, j * 128 : (j + 1) * 128] = total[k * 4 + j : k * 4 + j + 1, :]


def gate_sum(parts):
    return call(gate_sum_body, "gate_sum", None, [parts], [((2, 512), F32)])[0]


NEAREST = (0, 1, 7, 2, 6, 3, 5, 4)


def pack_body(*refs):
    for i, k in enumerate(NEAREST):
        refs[-1][k] = refs[i][...]


def pack(*pieces):
    return call(pack_body, "pack", None, pieces, [((NZ, EXPERTS, COLS, CAP), BF16)])[0]


SIDES = (0, 1, 3, 2)


def backward_body(where_ref, hidden_hbm, codes_hbm, scales_hbm, *rest):
    packs = rest[: NX + 1]
    hidden_out, weight_out, scale_out = rest[NX + 1 : NX + 4]
    hidden, codes, scales, grads, table, weight, sems = rest[NX + 4 :]
    units = hidden.shape[0]
    tiles = BLOCK // 128
    x_of = [lax.rem(where_ref[0] + side, NX) for side in SIDES]
    lanes_of = [pl.ds(pl.multiple_of(x * BLOCK, BLOCK), BLOCK) for x in x_of]
    head = [
        pltpu.make_async_copy(hidden_hbm, hidden, sems.at[0]),
        pltpu.make_async_copy(scales_hbm, scales, sems.at[1]),
    ]
    parts, arrive = [], []
    for n in range(NX):
        parts.append(pltpu.make_async_copy(codes_hbm.at[:, lanes_of[n]], codes.at[n], sems.at[2 + n]))
        arrive.append([])
        for k in range(NZ):
            z = lax.rem(where_ref[1] + k, NZ)
            rows = pl.ds(pl.multiple_of(n * BLOCK + z * COLS, COLS), COLS)
            source = packs[n].at[k] if n < NX - 1 else packs[n + k // 4].at[k % 4]
            arrive[n].append(pltpu.make_async_copy(source, grads.at[:, rows], sems.at[8 + n * NZ + k]))
    head[0].start()
    for copy in arrive[0]:
        copy.start()
    head[1].start()
    parts[0].start()
    for n in range(1, NX):
        for copy in arrive[n]:
            copy.start()
        parts[n].start()
    head[0].wait()
    head[1].wait()
    copies = []
    for n in range(NX):
        rows_here = slice(n * BLOCK, (n + 1) * BLOCK)
        for copy in arrive[n]:
            copy.wait()
        block = jnp.concatenate([grads[g, rows_here, :] for g in range(EXPERTS)], axis=1)
        slot = n % 2
        if n >= 2:
            copies[n - 2].wait()
        weight[slot] = lax.dot_general(
            hidden[...], block, (((1,), (1,)), ((), ())), preferred_element_type=F32
        )
        copies.append(pltpu.make_async_copy(weight.at[slot], weight_out.at[:, lanes_of[n]], sems.at[6 + slot]))
        copies[n].start()
        parts[n].wait()
        dequant(codes.at[n], scales, x_of[n] * tiles, table.at[:, rows_here])
        for g in range(units // GROUP):
            rows = slice(g * GROUP, (g + 1) * GROUP)
            line = jnp.sum(weight[slot, rows, :] * codes[n, rows, :].astype(F32), axis=0, keepdims=True)
            for j in range(tiles):
                row = (g * NX + x_of[n]) * tiles + j
                scale_out[pl.ds(row, 1), :] = line[:, j * 128 : (j + 1) * 128]
    block = jnp.concatenate([grads[g] for g in range(EXPERTS)], axis=1)
    hidden_out[...] = jnp.dot(table[...], block, preferred_element_type=F32).astype(BF16)
    copies[2].wait()
    copies[3].wait()


def backward(where, hidden, codes, scales, packs):
    units, slots = hidden.shape
    features = codes.shape[1]
    return pl.pallas_call(
        backward_body,
        in_specs=[SMEM] + [HBM] * (4 + NX),
        out_specs=[VMEM, HBM, VMEM],
        out_shape=[sds((units, slots), BF16), sds((units, features), F32), sds(scales.shape, F32)],
        scratch_shapes=[
            pltpu.VMEM((units, slots), BF16),
            pltpu.VMEM((NX, units, BLOCK), I32),
            pltpu.VMEM(scales.shape, F32),
            pltpu.VMEM((EXPERTS, features, CAP), BF16),
            pltpu.VMEM((units, features), BF16),
            pltpu.VMEM((2, units, BLOCK), F32),
            pltpu.SemaphoreType.DMA((8 + NX * NZ,)),
        ],
        compiler_params=LARGE,
        name="backward",
    )(where, *[away(a) for a in (hidden, codes, scales, *packs)])


def shift(value, axis, by):
    size = NX if axis == "x" else NZ
    return lax.ppermute(value, axis, [(i, (i + by) % size) for i in range(size)])


def on_device(hidden, weight_codes, group_scales, expert_index, gate_values, output_grad):
    weights = (hidden[0], weight_codes[0], group_scales.reshape(-1, 128))
    index, gate, grad = expert_index.T, gate_values.T, output_grad.T
    where = jnp.stack([lax.axis_index("x"), lax.axis_index("z")]).astype(I32)

    far_top, far_bottom = forward_far(where, *weights)
    far_top = shift(far_top, "x", 1)
    far_bottom = shift(far_bottom, "x", -1)

    place, outbound = slot_grads(index, gate, grad)
    shard = lax.all_to_all(outbound, ("y", "c"), 0, 0, tiled=True)
    far_top, far_bottom, shard = lax.optimization_barrier((far_top, far_bottom, shard))
    up, down = forward_join(where, *weights, far_top, far_bottom)
    where_late, up, down, shard = lax.optimization_barrier((where, up, down, shard))
    up = shift(up, "x", 1)
    down = shift(down, "x", -1)
    own = forward_own(where_late, *weights)
    along = [shift(shard, "z", -k) for k in NEAREST[1:]]

    ups, downs, far, up2, down2, rest = x_sum(where, own, up, down)
    rest, *along = lax.optimization_barrier((rest, *along))
    mine = pack(shard, *along)
    packs = [mine, shift(mine, "x", -1), shift(mine, "x", 1)]
    ups, downs, far = shift(ups, "z", 1), shift(downs, "z", -1), shift(far, "z", 2)
    up2, down2 = mid_sum(up2, down2, ups, downs, far)
    up2, down2 = shift(up2, "z", 2), shift(down2, "z", -2)
    up2, down2, packs[1], packs[2] = lax.optimization_barrier((up2, down2, packs[1], packs[2]))
    packs += [shift(packs[1][: NZ // 2], "x", -1), shift(packs[2][NZ // 2 :], "x", 1)]
    returned = lax.all_to_all(z_sum(rest, ups, downs, up2, down2), ("y", "c"), 0, 0, tiled=True)
    combined, spread = combine(place, gate, grad, returned)
    gate_parts = lax.all_to_all(spread, ("x", "z"), 0, 0, tiled=True)
    hidden_grad, weight_grad, scale_grad = backward(where, *weights, packs)
    gate_parts, hidden_grad = lax.optimization_barrier((gate_parts, hidden_grad))
    gate_grad = gate_sum(gate_parts)
    return combined.T, gate_grad.T, hidden_grad[None], weight_grad[None], scale_grad.reshape(group_scales.shape)


def solution(mesh):
    fine = Mesh(mesh.devices.reshape(NY, NC, NX, NZ), ("y", "c", "x", "z"))
    expert, dp = ("y", "c"), ("x", "z")
    return jax.shard_map(
        on_device,
        mesh=fine,
        in_specs=(
            P(expert, dp, None),
            P(expert, dp, None),
            P(expert, dp, None),
            P(expert, None),
            P(expert, None),
            P(expert, dp),
        ),
        out_specs=(
            P(expert, dp),
            P(expert, None),
            P(expert, dp, None),
            P(expert, dp, None),
            P(expert, dp, None),
        ),
        check_vma=False,
    )
```

```python
import jax
import jax.numpy as jnp
from jax import lax
from jax.experimental import pallas as pl
from jax.experimental.pallas import tpu as pltpu
from jax.sharding import Mesh, PartitionSpec as P

EXPERTS = 8
GROUP = 32
CAP = 128
NY, NC, NX, NZ = 4, 2, 4, 8
COLS = 64
SLOTS = EXPERTS * CAP
BLOCK = NZ * COLS
SMALL = pltpu.CompilerParams(vmem_limit_bytes=16 * 1024 * 1024)
LARGE = pltpu.CompilerParams(vmem_limit_bytes=32 * 1024 * 1024)
F32, BF16, I32 = jnp.float32, jnp.bfloat16, jnp.int32


sds = jax.ShapeDtypeStruct
HBM, VMEM, SMEM = (pl.BlockSpec(memory_space=m) for m in (pltpu.HBM, pltpu.VMEM, pltpu.SMEM))


def near(array):
    return pltpu.with_memory_space_constraint(array, pltpu.VMEM)


def away(array):
    return pltpu.with_memory_space_constraint(array, pltpu.HBM)


def call(body, name, where, operands, outs, scratch=(), far=()):
    heads = [] if where is None else [where]
    return pl.pallas_call(
        body,
        in_specs=[SMEM] * len(heads) + [HBM] * len(far) + [VMEM] * len(operands),
        out_specs=[VMEM] * len(outs),
        out_shape=[pltpu.VMEM(shape, dtype) for shape, dtype in outs],
        scratch_shapes=list(scratch),
        compiler_params=SMALL,
        name=name,
    )(*heads, *[away(a) for a in far], *[near(a) for a in operands])


def dequant(codes_ref, scales_ref, tile, table_ref):
    units, width = codes_ref.shape
    tiles = scales_ref.shape[0] // (units // GROUP)
    for j in range(width // 128):
        lanes = slice(j * 128, (j + 1) * 128)
        for g in range(units // GROUP):
            rows = slice(g * GROUP, (g + 1) * GROUP)
            scale = scales_ref[pl.ds(g * tiles + tile + j, 1), :]
            table_ref[rows, lanes] = (codes_ref[rows, lanes].astype(F32) * scale).astype(BF16)


def picker(place_ref, k):
    slots = lax.broadcasted_iota(I32, (SLOTS, place_ref.shape[1]), 0)
    return (place_ref[k : k + 1, :] == slots).astype(BF16)


def slot_body(index_ref, gate_ref, grad_ref, place_ref, out_ref):
    tokens = index_ref.shape[1]
    experts = lax.broadcasted_iota(I32, (EXPERTS, tokens), 0)
    hot = [(index_ref[k : k + 1, :] == experts).astype(F32) for k in range(2)]
    row = lax.broadcasted_iota(I32, (tokens, tokens), 0)
    col = lax.broadcasted_iota(I32, (tokens, tokens), 1)
    before = (row < col).astype(BF16)
    counts = jnp.dot((hot[0] + hot[1]).astype(BF16), before, preferred_element_type=F32)
    for k in range(2):
        rank = jnp.sum(counts * hot[k], axis=0, keepdims=True).astype(I32)
        place_ref[k : k + 1, :] = jnp.where(rank < CAP, index_ref[k : k + 1, :] * CAP + rank, -1)
    grad = grad_ref[...].astype(F32)
    total = None
    for k in range(2):
        value = (gate_ref[k : k + 1, :] * grad).astype(BF16)
        piece = lax.dot_general(
            value, picker(place_ref, k), (((1,), (1,)), ((), ())), preferred_element_type=F32
        )
        total = piece if total is None else total + piece
    total = total.astype(BF16)
    for e in range(EXPERTS):
        out_ref[e] = total[:, e * CAP : (e + 1) * CAP]


def slot_grads(index, gate, grad):
    outs = [(index.shape, I32), ((EXPERTS, COLS, CAP), BF16)]
    return call(slot_body, "slot_grads", None, [index, gate, grad], outs)


def loads(where_ref, hops, hidden_hbm, codes_hbm, scales_hbm, hidden, codes, scales, sems):
    copies = [
        pltpu.make_async_copy(scales_hbm, scales, sems.at[0]),
        pltpu.make_async_copy(hidden_hbm, hidden, sems.at[1]),
    ]
    for i, hop in enumerate(hops):
        start = pl.multiple_of(lax.rem(where_ref[0] + hop, NX) * BLOCK, BLOCK)
        copies.append(pltpu.make_async_copy(codes_hbm.at[:, pl.ds(start, BLOCK)], codes.at[i], sems.at[2 + i]))
    for copy in copies:
        copy.start()
    copies[0].wait()
    return copies[1:]


def buffers(units, count):
    return [
        pltpu.VMEM((units, SLOTS), BF16),
        pltpu.VMEM((count, units, BLOCK), I32),
        pltpu.VMEM((units // GROUP * (NX * BLOCK // 128), 128), F32),
        pltpu.VMEM((units, BLOCK), BF16),
        pltpu.SemaphoreType.DMA((2 + count,)),
    ]


def block_value(where_ref, hops, hidden, codes, scales, table, copy, others=()):
    copy.wait()
    dequant(codes, scales, lax.rem(where_ref[0] + hops, NX) * (BLOCK // 128), table)
    for other in others:
        other.wait()
    return lax.dot_general(table[...], hidden[...], (((0,), (0,)), ((), ())), preferred_element_type=F32)


def far_body(where_ref, hidden_hbm, codes_hbm, scales_hbm, top_ref, bottom_ref, hidden, codes, scales, table, sems):
    first, *copies = loads(where_ref, (2,), hidden_hbm, codes_hbm, scales_hbm, hidden, codes, scales, sems)
    value = block_value(where_ref, 2, hidden, codes.at[0], scales, table, copies[0], (first,)).astype(BF16)
    top_ref[...] = value[: BLOCK // 2]
    bottom_ref[...] = value[BLOCK // 2 :]


def forward_far(where, *arrays):
    half = ((BLOCK // 2, SLOTS), BF16)
    return call(far_body, "forward_far", where, [], [half, half], buffers(arrays[0].shape[0], 1), arrays)


def join_body(
    where_ref, hidden_hbm, codes_hbm, scales_hbm, top_ref, bottom_ref, up_ref, down_ref, hidden, codes, scales, table, sems
):
    first, *copies = loads(where_ref, (1, 3), hidden_hbm, codes_hbm, scales_hbm, hidden, codes, scales, sems)
    half = BLOCK // 2
    value = block_value(where_ref, 1, hidden, codes.at[0], scales, table, copies[0], (first,))
    up_ref[:half] = (value[:half] + top_ref[...].astype(F32)).astype(BF16)
    up_ref[half:] = value[half:].astype(BF16)
    value = block_value(where_ref, 3, hidden, codes.at[1], scales, table, copies[1])
    down_ref[:half] = value[:half].astype(BF16)
    down_ref[half:] = (value[half:] + bottom_ref[...].astype(F32)).astype(BF16)


def forward_join(where, hidden, codes, scales, top, bottom):
    outs = [((BLOCK, SLOTS), BF16)] * 2
    far = (hidden, codes, scales)
    return call(join_body, "forward_join", where, [top, bottom], outs, buffers(hidden.shape[0], 2), far)


def own_body(where_ref, hidden_hbm, codes_hbm, scales_hbm, own_ref, hidden, codes, scales, table, sems):
    first, *copies = loads(where_ref, (0,), hidden_hbm, codes_hbm, scales_hbm, hidden, codes, scales, sems)
    own_ref[...] = block_value(where_ref, 0, hidden, codes.at[0], scales, table, copies[0], (first,))


def forward_own(where, *arrays):
    outs = [((BLOCK, SLOTS), F32)]
    return call(own_body, "forward_own", where, [], outs, buffers(arrays[0].shape[0], 1), arrays)[0]


def x_sum_body(where_ref, own_ref, up_ref, down_ref, ups_ref, downs_ref, far_ref, up2_ref, down2_ref, rest_ref):
    def total(hops):
        rows = pl.ds(pl.multiple_of(lax.rem(where_ref[1] + hops, NZ) * COLS, COLS), COLS)
        return own_ref[rows, :] + up_ref[rows, :].astype(F32) + down_ref[rows, :].astype(F32)

    ups_ref[0] = total(3).astype(BF16)
    ups_ref[1] = total(1).astype(BF16)
    downs_ref[0] = total(5).astype(BF16)
    downs_ref[1] = total(7).astype(BF16)
    far_ref[...] = total(4).astype(BF16)
    up2_ref[...] = total(2)
    down2_ref[...] = total(6)
    rest_ref[...] = total(0)


def x_sum(where, *arrays):
    one, two = (COLS, SLOTS), (2, COLS, SLOTS)
    outs = [(two, BF16), (two, BF16), (one, BF16), (one, F32), (one, F32), (one, F32)]
    return call(x_sum_body, "x_sum", where, arrays, outs)


def mid_sum_body(up2_ref, down2_ref, ups_ref, downs_ref, far_ref, up_out, down_out):
    up_out[...] = (up2_ref[...] + ups_ref[0].astype(F32) + far_ref[...].astype(F32)).astype(BF16)
    down_out[...] = (down2_ref[...] + downs_ref[0].astype(F32)).astype(BF16)


def mid_sum(*arrays):
    return call(mid_sum_body, "mid_sum", None, arrays, [((COLS, SLOTS), BF16)] * 2)


def z_sum_body(rest_ref, ups_ref, downs_ref, up_ref, down_ref, out_ref):
    total = rest_ref[...] + ups_ref[1].astype(F32) + downs_ref[1].astype(F32)
    total = (total + up_ref[...].astype(F32) + down_ref[...].astype(F32)).astype(BF16)
    for g in range(EXPERTS):
        out_ref[g] = total[:, g * CAP : (g + 1) * CAP]


def z_sum(*arrays):
    return call(z_sum_body, "z_sum", None, arrays, [((EXPERTS, COLS, CAP), BF16)])[0]


def combine_body(place_ref, gate_ref, grad_ref, back_ref, out_ref, spread_ref):
    back = jnp.concatenate([back_ref[e] for e in range(EXPERTS)], axis=1)
    grad = grad_ref[...].astype(F32)
    total = None
    for k in range(2):
        got = jnp.dot(back, picker(place_ref, k), preferred_element_type=F32)
        piece = gate_ref[k : k + 1, :] * got
        total = piece if total is None else total + piece
        part = jnp.sum(grad * got, axis=0, keepdims=True)
        for j in range(4):
            line = part[:, j * 128 : (j + 1) * 128]
            spread_ref[:, k * 4 + j : k * 4 + j + 1, :] = jnp.broadcast_to(line[None], (NX * NZ, 1, 128))
    out_ref[...] = total.astype(BF16)


def combine(place, gate, grad, back):
    outs = [(grad.shape, BF16), ((NX * NZ, 8, 128), F32)]
    return call(combine_body, "combine", None, [place, gate, grad, back], outs)


def gate_sum_body(parts_ref, out_ref):
    total = jnp.sum(parts_ref[...], axis=0)
    for k in range(2):
        for j in range(4):
            out_ref[k : k + 1, j * 128 : (j + 1) * 128] = total[k * 4 + j : k * 4 + j + 1, :]


def gate_sum(parts):
    return call(gate_sum_body, "gate_sum", None, [parts], [((2, 512), F32)])[0]


NEAREST = (0, 1, 7, 2, 6, 3, 5, 4)


def pack_body(*refs):
    for i, k in enumerate(NEAREST):
        refs[-1][k] = refs[i][...]


def pack(*pieces):
    return call(pack_body, "pack", None, pieces, [((NZ, EXPERTS, COLS, CAP), BF16)])[0]


def backward(where, hidden, codes, scales, packs, sides, before=()):
    units, slots = hidden.shape
    features = codes.shape[1]
    count, tiles = len(sides), BLOCK // 128
    operands = [hidden, codes, scales, *packs, *before]

    def body(where_ref, hidden_hbm, codes_hbm, scales_hbm, *rest):
        packs_hbm, rest = rest[: len(packs)], rest[len(packs) :]
        before_hbm, rest = rest[: len(before)], rest[len(before) :]
        hidden_out, weight_out, scale_out, hidden_v, codes_v, scales_v, grads, table, weight, acc, sems = rest
        x_of = [lax.rem(where_ref[0] + side, NX) for side in sides]
        lanes_of = [pl.ds(pl.multiple_of(x * BLOCK, BLOCK), BLOCK) for x in x_of]
        head = [
            pltpu.make_async_copy(hidden_hbm, hidden_v, sems.at[0]),
            pltpu.make_async_copy(scales_hbm, scales_v, sems.at[1]),
        ]
        if before:
            head.append(pltpu.make_async_copy(before_hbm[0], acc, sems.at[2]))
            head.append(pltpu.make_async_copy(before_hbm[2], scale_out, sems.at[3]))
        parts, arrive = [], []
        for n in range(count):
            parts.append(pltpu.make_async_copy(codes_hbm.at[:, lanes_of[n]], codes_v.at[n], sems.at[8 + n]))
            arrive.append([])
            for k in range(NZ):
                z = lax.rem(where_ref[1] + k, NZ)
                rows = pl.ds(pl.multiple_of(n * BLOCK + z * COLS, COLS), COLS)
                per = NZ * count // len(packs)
                source = packs_hbm[(n * NZ + k) // per].at[(n * NZ + k) % per]
                sem = sems.at[8 + count + n * NZ + k]
                arrive[n].append(pltpu.make_async_copy(source, grads.at[:, rows], sem))
        head[0].start()
        for copy in arrive[0]:
            copy.start()
        for copy in head[1:]:
            copy.start()
        parts[0].start()
        for n in range(1, count):
            for copy in arrive[n]:
                copy.start()
            parts[n].start()
        for copy in head:
            copy.wait()
        copies = []
        for n in range(count):
            rows_here = slice(n * BLOCK, (n + 1) * BLOCK)
            for copy in arrive[n]:
                copy.wait()
            block = jnp.concatenate([grads[g, rows_here, :] for g in range(EXPERTS)], axis=1)
            weight[n] = lax.dot_general(
                hidden_v[...], block, (((1,), (1,)), ((), ())), preferred_element_type=F32
            )
            copies.append(pltpu.make_async_copy(weight.at[n], weight_out.at[:, lanes_of[n]], sems.at[4 + n]))
            copies[n].start()
            parts[n].wait()
            dequant(codes_v.at[n], scales_v, x_of[n] * tiles, table.at[:, rows_here])
            for g in range(units // GROUP):
                rows = slice(g * GROUP, (g + 1) * GROUP)
                line = jnp.sum(weight[n, rows, :] * codes_v[n, rows, :].astype(F32), axis=0, keepdims=True)
                for j in range(tiles):
                    row = (g * NX + x_of[n]) * tiles + j
                    scale_out[pl.ds(row, 1), :] = line[:, j * 128 : (j + 1) * 128]
        block = jnp.concatenate([grads[g] for g in range(EXPERTS)], axis=1)
        value = jnp.dot(table[...], block, preferred_element_type=F32)
        if before:
            value = value + acc[...]
        hidden_out[...] = value.astype(hidden_out.dtype)
        for copy in copies:
            copy.wait()

    first = 1 + len(operands) - len(before)
    return pl.pallas_call(
        body,
        in_specs=[SMEM] + [HBM] * len(operands),
        out_specs=[VMEM, HBM, VMEM],
        out_shape=[sds((units, slots), BF16 if before else F32), sds((units, features), F32), sds(scales.shape, F32)],
        input_output_aliases={first + 1: 1} if before else {},
        scratch_shapes=[
            pltpu.VMEM((units, slots), BF16),
            pltpu.VMEM((count, units, BLOCK), I32),
            pltpu.VMEM(scales.shape, F32),
            pltpu.VMEM((EXPERTS, count * BLOCK, CAP), BF16),
            pltpu.VMEM((units, count * BLOCK), BF16),
            pltpu.VMEM((count, units, BLOCK), F32),
            pltpu.VMEM((units, slots), F32),
            pltpu.SemaphoreType.DMA((8 + count + count * NZ,)),
        ],
        compiler_params=LARGE,
        name="backward_last" if before else "backward_first",
    )(where, *[away(a) for a in operands])


def shift(value, axis, by):
    size = NX if axis == "x" else NZ
    return lax.ppermute(value, axis, [(i, (i + by) % size) for i in range(size)])


def on_device(hidden, weight_codes, group_scales, expert_index, gate_values, output_grad):
    weights = (hidden[0], weight_codes[0], group_scales.reshape(-1, 128))
    index, gate, grad = expert_index.T, gate_values.T, output_grad.T
    where = jnp.stack([lax.axis_index("x"), lax.axis_index("z")]).astype(I32)

    far_top, far_bottom = forward_far(where, *weights)
    far_top = shift(far_top, "x", 1)
    far_bottom = shift(far_bottom, "x", -1)

    place, outbound = slot_grads(index, gate, grad)
    shard = lax.all_to_all(outbound, ("y", "c"), 0, 0, tiled=True)
    far_top, far_bottom, shard = lax.optimization_barrier((far_top, far_bottom, shard))
    up, down = forward_join(where, *weights, far_top, far_bottom)
    where_late, up, down, shard = lax.optimization_barrier((where, up, down, shard))
    up = shift(up, "x", 1)
    down = shift(down, "x", -1)
    own = forward_own(where_late, *weights)
    along = [shift(shard, "z", -k) for k in NEAREST[4:]]
    own, shard_late = lax.optimization_barrier((own, shard))
    along = [shift(shard_late, "z", -k) for k in NEAREST[1:4]] + along

    ups, downs, far, up2, down2, rest = x_sum(where, own, up, down)
    rest, *along = lax.optimization_barrier((rest, *along))
    mine = pack(shard, *along)
    packs = [mine, shift(mine, "x", -1), shift(mine, "x", 1)]
    ups, downs, far = shift(ups, "z", 1), shift(downs, "z", -1), shift(far, "z", 2)
    up2, down2 = mid_sum(up2, down2, ups, downs, far)
    up2, down2 = shift(up2, "z", 2), shift(down2, "z", -2)
    summed = z_sum(rest, ups, downs, up2, down2)
    summed, packs[1], packs[2] = lax.optimization_barrier((summed, packs[1], packs[2]))
    opposite = [shift(packs[1][: NZ // 2], "x", -1), shift(packs[2][NZ // 2 :], "x", 1)]
    returned = lax.all_to_all(summed, ("y", "c"), 0, 0, tiled=True)
    begun = backward(where, *weights, packs, (0, 1, 3))
    returned, *begun = lax.optimization_barrier((returned, *begun))
    combined, spread = combine(place, gate, grad, returned)
    gate_parts = lax.all_to_all(spread, ("x", "z"), 0, 0, tiled=True)
    hidden_grad, weight_grad, scale_grad = backward(where, *weights, opposite, (2,), begun)
    gate_parts, hidden_grad = lax.optimization_barrier((gate_parts, hidden_grad))
    gate_grad = gate_sum(gate_parts)
    return combined.T, gate_grad.T, hidden_grad[None], weight_grad[None], scale_grad.reshape(group_scales.shape)


def solution(mesh):
    fine = Mesh(mesh.devices.reshape(NY, NC, NX, NZ), ("y", "c", "x", "z"))
    expert, dp = ("y", "c"), ("x", "z")
    return jax.shard_map(
        on_device,
        mesh=fine,
        in_specs=(
            P(expert, dp, None),
            P(expert, dp, None),
            P(expert, dp, None),
            P(expert, None),
            P(expert, None),
            P(expert, dp),
        ),
        out_specs=(
            P(expert, dp),
            P(expert, None),
            P(expert, dp, None),
            P(expert, dp, None),
            P(expert, dp, None),
        ),
        check_vma=False,
    )
```

```python
import jax
import jax.numpy as jnp
from jax import lax
from jax.experimental import pallas as pl
from jax.experimental.pallas import tpu as pltpu
from jax.sharding import Mesh, PartitionSpec as P

EXPERTS = 8
GROUP = 32
CAP = 128
NY, NC, NX, NZ = 4, 2, 4, 8
COLS = 64
SLOTS = EXPERTS * CAP
BLOCK = NZ * COLS
SMALL = pltpu.CompilerParams(vmem_limit_bytes=16 * 1024 * 1024)
LARGE = pltpu.CompilerParams(vmem_limit_bytes=32 * 1024 * 1024)
F32, BF16, I32 = jnp.float32, jnp.bfloat16, jnp.int32


sds = jax.ShapeDtypeStruct
HBM, VMEM, SMEM = (pl.BlockSpec(memory_space=m) for m in (pltpu.HBM, pltpu.VMEM, pltpu.SMEM))


def near(array):
    return pltpu.with_memory_space_constraint(array, pltpu.VMEM)


def away(array):
    return pltpu.with_memory_space_constraint(array, pltpu.HBM)


def call(body, name, where, operands, outs, scratch=(), far=(), keep=None):
    heads = [] if where is None else [where]
    keep = len(outs) if keep is None else keep
    return pl.pallas_call(
        body,
        in_specs=[SMEM] * len(heads) + [HBM] * len(far) + [VMEM] * len(operands),
        out_specs=[VMEM] * len(outs),
        out_shape=[(pltpu.VMEM if i < keep else sds)(*out) for i, out in enumerate(outs)],
        scratch_shapes=list(scratch),
        compiler_params=SMALL,
        name=name,
    )(*heads, *[away(a) for a in far], *[near(a) for a in operands])


def dequant(codes_ref, scales_ref, tile, table_ref):
    units, width = codes_ref.shape
    tiles = scales_ref.shape[0] // (units // GROUP)
    for j in range(width // 128):
        lanes = slice(j * 128, (j + 1) * 128)
        for g in range(units // GROUP):
            rows = slice(g * GROUP, (g + 1) * GROUP)
            scale = scales_ref[pl.ds(g * tiles + tile + j, 1), :]
            table_ref[rows, lanes] = (codes_ref[rows, lanes].astype(F32) * scale).astype(BF16)


def picker(place_ref, k):
    slots = lax.broadcasted_iota(I32, (SLOTS, place_ref.shape[1]), 0)
    return (place_ref[k : k + 1, :] == slots).astype(BF16)


def slot_body(index_ref, gate_ref, grad_ref, place_ref, out_ref):
    tokens = index_ref.shape[1]
    experts = lax.broadcasted_iota(I32, (EXPERTS, tokens), 0)
    hot = [(index_ref[k : k + 1, :] == experts).astype(F32) for k in range(2)]
    row = lax.broadcasted_iota(I32, (tokens, tokens), 0)
    col = lax.broadcasted_iota(I32, (tokens, tokens), 1)
    before = (row < col).astype(BF16)
    counts = jnp.dot((hot[0] + hot[1]).astype(BF16), before, preferred_element_type=F32)
    for k in range(2):
        rank = jnp.sum(counts * hot[k], axis=0, keepdims=True).astype(I32)
        place_ref[k : k + 1, :] = jnp.where(rank < CAP, index_ref[k : k + 1, :] * CAP + rank, -1)
    grad = grad_ref[...].astype(F32)
    total = None
    for k in range(2):
        value = (gate_ref[k : k + 1, :] * grad).astype(BF16)
        piece = lax.dot_general(
            value, picker(place_ref, k), (((1,), (1,)), ((), ())), preferred_element_type=F32
        )
        total = piece if total is None else total + piece
    total = total.astype(BF16)
    for e in range(EXPERTS):
        out_ref[e] = total[:, e * CAP : (e + 1) * CAP]


def slot_grads(index, gate, grad):
    outs = [(index.shape, I32), ((EXPERTS, COLS, CAP), BF16)]
    return call(slot_body, "slot_grads", None, [index, gate, grad], outs)


def loads(where_ref, hops, hidden_hbm, codes_hbm, scales_hbm, hidden, codes, scales, sems):
    copies = [
        pltpu.make_async_copy(scales_hbm, scales, sems.at[0]),
        pltpu.make_async_copy(hidden_hbm, hidden, sems.at[1]),
    ]
    for i, hop in enumerate(hops):
        start = pl.multiple_of(lax.rem(where_ref[0] + hop, NX) * BLOCK, BLOCK)
        copies.append(pltpu.make_async_copy(codes_hbm.at[:, pl.ds(start, BLOCK)], codes.at[i], sems.at[2 + i]))
    for copy in copies:
        copy.start()
    copies[0].wait()
    return copies[1:]


def buffers(units, count):
    return [
        pltpu.VMEM((units, SLOTS), BF16),
        pltpu.VMEM((count, units, BLOCK), I32),
        pltpu.VMEM((units // GROUP * (NX * BLOCK // 128), 128), F32),
        pltpu.VMEM((units, BLOCK), BF16),
        pltpu.SemaphoreType.DMA((2 + count,)),
    ]


def block_value(where_ref, hops, hidden, codes, scales, table, copy, others=()):
    copy.wait()
    dequant(codes, scales, lax.rem(where_ref[0] + hops, NX) * (BLOCK // 128), table)
    for other in others:
        other.wait()
    return lax.dot_general(table[...], hidden[...], (((0,), (0,)), ((), ())), preferred_element_type=F32)


def far_body(where_ref, hidden_hbm, codes_hbm, scales_hbm, top_ref, bottom_ref, hidden, codes, scales, table, sems):
    first, *copies = loads(where_ref, (2,), hidden_hbm, codes_hbm, scales_hbm, hidden, codes, scales, sems)
    value = block_value(where_ref, 2, hidden, codes.at[0], scales, table, copies[0], (first,)).astype(BF16)
    top_ref[...] = value[: BLOCK // 2]
    bottom_ref[...] = value[BLOCK // 2 :]


def forward_far(where, *arrays):
    half = ((BLOCK // 2, SLOTS), BF16)
    return call(far_body, "forward_far", where, [], [half, half], buffers(arrays[0].shape[0], 1), arrays)


def join_body(
    where_ref, hidden_hbm, codes_hbm, scales_hbm, top_ref, bottom_ref, up_ref, down_ref, own_ref, hidden, codes, scales, table, sems
):
    first, *copies = loads(where_ref, (1, 3, 0), hidden_hbm, codes_hbm, scales_hbm, hidden, codes, scales, sems)
    half = BLOCK // 2
    value = block_value(where_ref, 1, hidden, codes.at[0], scales, table, copies[0], (first,))
    up_ref[:half] = (value[:half] + top_ref[...].astype(F32)).astype(BF16)
    up_ref[half:] = value[half:].astype(BF16)
    value = block_value(where_ref, 3, hidden, codes.at[1], scales, table, copies[1])
    down_ref[:half] = value[:half].astype(BF16)
    down_ref[half:] = (value[half:] + bottom_ref[...].astype(F32)).astype(BF16)
    own_ref[...] = block_value(where_ref, 0, hidden, codes.at[2], scales, table, copies[2])


def forward_join(where, hidden, codes, scales, top, bottom):
    outs = [((BLOCK, SLOTS), BF16)] * 2 + [((BLOCK, SLOTS), F32)]
    far = (hidden, codes, scales)
    return call(join_body, "forward_join", where, [top, bottom], outs, buffers(hidden.shape[0], 3), far)


def x_sum_body(where_ref, own_ref, up_ref, down_ref, ups_ref, downs_ref, far_ref, up2_ref, down2_ref, rest_ref):
    def total(hops):
        rows = pl.ds(pl.multiple_of(lax.rem(where_ref[1] + hops, NZ) * COLS, COLS), COLS)
        return own_ref[rows, :] + up_ref[rows, :].astype(F32) + down_ref[rows, :].astype(F32)

    ups_ref[0] = total(3).astype(BF16)
    ups_ref[1] = total(1).astype(BF16)
    downs_ref[0] = total(5).astype(BF16)
    downs_ref[1] = total(7).astype(BF16)
    far_ref[...] = total(4).astype(BF16)
    up2_ref[...] = total(2)
    down2_ref[...] = total(6)
    rest_ref[...] = total(0)


def x_sum(where, *arrays):
    one, two = (COLS, SLOTS), (2, COLS, SLOTS)
    outs = [(two, BF16), (two, BF16), (one, BF16), (one, F32), (one, F32), (one, F32)]
    return call(x_sum_body, "x_sum", where, arrays, outs)


def mid_sum_body(up2_ref, down2_ref, ups_ref, downs_ref, far_ref, up_out, down_out):
    up_out[...] = (up2_ref[...] + ups_ref[0].astype(F32) + far_ref[...].astype(F32)).astype(BF16)
    down_out[...] = (down2_ref[...] + downs_ref[0].astype(F32)).astype(BF16)


def mid_sum(*arrays):
    return call(mid_sum_body, "mid_sum", None, arrays, [((COLS, SLOTS), BF16)] * 2)


def z_sum_body(rest_ref, ups_ref, downs_ref, up_ref, down_ref, out_ref):
    total = rest_ref[...] + ups_ref[1].astype(F32) + downs_ref[1].astype(F32)
    total = (total + up_ref[...].astype(F32) + down_ref[...].astype(F32)).astype(BF16)
    for g in range(EXPERTS):
        out_ref[g] = total[:, g * CAP : (g + 1) * CAP]


def z_sum(*arrays):
    return call(z_sum_body, "z_sum", None, arrays, [((EXPERTS, COLS, CAP), BF16)])[0]


def combine_body(place_ref, gate_ref, grad_ref, back_ref, spread_ref, out_ref):
    back = jnp.concatenate([back_ref[e] for e in range(EXPERTS)], axis=1)
    grad = grad_ref[...].astype(F32)
    total = None
    for k in range(2):
        got = jnp.dot(back, picker(place_ref, k), preferred_element_type=F32)
        piece = gate_ref[k : k + 1, :] * got
        total = piece if total is None else total + piece
        part = jnp.sum(grad * got, axis=0, keepdims=True)
        for j in range(4):
            line = part[:, j * 128 : (j + 1) * 128]
            spread_ref[:, k * 4 + j : k * 4 + j + 1, :] = jnp.broadcast_to(line[None], (NX * NZ, 1, 128))
    out_ref[...] = total.astype(BF16)


def combine(place, gate, grad, back):
    outs = [((NX * NZ, 8, 128), F32), (grad.shape, BF16)]
    return call(combine_body, "combine", None, [place, gate, grad, back], outs, keep=1)


def gate_sum_body(parts_ref, out_ref):
    total = jnp.sum(parts_ref[...], axis=0)
    for k in range(2):
        for j in range(4):
            out_ref[k : k + 1, j * 128 : (j + 1) * 128] = total[k * 4 + j : k * 4 + j + 1, :]


def gate_sum(parts):
    return call(gate_sum_body, "gate_sum", None, [parts], [((2, 512), F32)], keep=0)[0]


NEAREST = (0, 1, 7, 2, 6, 3, 5, 4)


def pack_body(*refs):
    for i, k in enumerate(NEAREST):
        refs[-1][k] = refs[i][...]


def pack(*pieces):
    return call(pack_body, "pack", None, pieces, [((NZ, EXPERTS, COLS, CAP), BF16)])[0]


SIDES = (0, 1, 3, 2)


def backward(where, hidden, codes, scales, packs):
    units, slots = hidden.shape
    features = codes.shape[1]
    count, tiles = NX, BLOCK // 128
    operands = [hidden, codes, scales, *packs]

    def body(where_ref, hidden_hbm, codes_hbm, scales_hbm, *rest):
        packs_hbm, rest = rest[: len(packs)], rest[len(packs) :]
        hidden_out, weight_out, scale_out, hidden_v, codes_v, scales_v, grads, table, weight, sems = rest
        x_of = [lax.rem(where_ref[0] + side, NX) for side in SIDES]
        lanes_of = [pl.ds(pl.multiple_of(x * BLOCK, BLOCK), BLOCK) for x in x_of]
        head = [
            pltpu.make_async_copy(hidden_hbm, hidden_v, sems.at[0]),
            pltpu.make_async_copy(scales_hbm, scales_v, sems.at[1]),
        ]
        parts, arrive = [], []
        for n in range(count):
            parts.append(pltpu.make_async_copy(codes_hbm.at[:, lanes_of[n]], codes_v.at[n], sems.at[8 + n]))
            arrive.append([])
            for k in range(NZ):
                z = lax.rem(where_ref[1] + k, NZ)
                rows = pl.ds(pl.multiple_of(n * BLOCK + z * COLS, COLS), COLS)
                source = packs_hbm[n].at[k]
                sem = sems.at[8 + count + n * NZ + k]
                arrive[n].append(pltpu.make_async_copy(source, grads.at[:, rows], sem))
        head[0].start()
        for copy in arrive[0]:
            copy.start()
        for copy in head[1:]:
            copy.start()
        parts[0].start()
        for n in range(1, count):
            for copy in arrive[n]:
                copy.start()
            parts[n].start()
        for copy in head:
            copy.wait()
        copies = []
        for n in range(count):
            rows_here = slice(n * BLOCK, (n + 1) * BLOCK)
            for copy in arrive[n]:
                copy.wait()
            block = jnp.concatenate([grads[g, rows_here, :] for g in range(EXPERTS)], axis=1)
            weight[n] = lax.dot_general(
                hidden_v[...], block, (((1,), (1,)), ((), ())), preferred_element_type=F32
            )
            copies.append(pltpu.make_async_copy(weight.at[n], weight_out.at[:, lanes_of[n]], sems.at[4 + n]))
            copies[n].start()
            parts[n].wait()
            dequant(codes_v.at[n], scales_v, x_of[n] * tiles, table.at[:, rows_here])
            for g in range(units // GROUP):
                rows = slice(g * GROUP, (g + 1) * GROUP)
                line = jnp.sum(weight[n, rows, :] * codes_v[n, rows, :].astype(F32), axis=0, keepdims=True)
                for j in range(tiles):
                    row = (g * NX + x_of[n]) * tiles + j
                    scale_out[pl.ds(row, 1), :] = line[:, j * 128 : (j + 1) * 128]
        block = jnp.concatenate([grads[g] for g in range(EXPERTS)], axis=1)
        hidden_out[...] = jnp.dot(table[...], block, preferred_element_type=F32).astype(BF16)
        for copy in copies:
            copy.wait()

    return pl.pallas_call(
        body,
        in_specs=[SMEM] + [HBM] * len(operands),
        out_specs=[VMEM, HBM, VMEM],
        out_shape=[sds((units, slots), BF16), sds((units, features), F32), sds(scales.shape, F32)],
        scratch_shapes=[
            pltpu.VMEM((units, slots), BF16),
            pltpu.VMEM((count, units, BLOCK), I32),
            pltpu.VMEM(scales.shape, F32),
            pltpu.VMEM((EXPERTS, count * BLOCK, CAP), BF16),
            pltpu.VMEM((units, count * BLOCK), BF16),
            pltpu.VMEM((count, units, BLOCK), F32),
            pltpu.SemaphoreType.DMA((8 + count + count * NZ,)),
        ],
        compiler_params=LARGE,
        name="backward",
    )(where, *[away(a) for a in operands])


def shift(value, axis, by):
    size = NX if axis == "x" else NZ
    return lax.ppermute(value, axis, [(i, (i + by) % size) for i in range(size)])


def on_device(hidden, weight_codes, group_scales, expert_index, gate_values, output_grad):
    weights = (hidden[0], weight_codes[0], group_scales.reshape(-1, 128))
    index, gate, grad = expert_index.T, gate_values.T, output_grad.T
    where = jnp.stack([lax.axis_index("x"), lax.axis_index("z")]).astype(I32)

    far_top, far_bottom = forward_far(where, *weights)
    far_top = shift(far_top, "x", 1)
    far_bottom = shift(far_bottom, "x", -1)

    place, outbound = slot_grads(index, gate, grad)
    shard = lax.all_to_all(outbound, ("y", "c"), 0, 0, tiled=True)
    far_top, far_bottom, shard = lax.optimization_barrier((far_top, far_bottom, shard))
    up, down, own = forward_join(where, *weights, far_top, far_bottom)
    up, down, shard = lax.optimization_barrier((up, down, shard))
    up = shift(up, "x", 1)
    down = shift(down, "x", -1)
    along = [shift(shard, "z", -k) for k in NEAREST[1:]]
    up, down, *along[4:] = lax.optimization_barrier((up, down, *along[4:]))

    ups, downs, far, up2, down2, rest = x_sum(where, own, up, down)
    rest, *along = lax.optimization_barrier((rest, *along))
    mine = pack(shard, *along)
    packs = [mine, shift(mine, "x", -1), shift(mine, "x", 1)]
    ups, downs, far = shift(ups, "z", 1), shift(downs, "z", -1), shift(far, "z", 2)
    up2, down2 = mid_sum(up2, down2, ups, downs, far)
    up2, down2, mine = lax.optimization_barrier((up2, down2, mine))
    packs.append(shift(mine, "x", 2))
    up2, down2 = shift(up2, "z", 2), shift(down2, "z", -2)
    returned = lax.all_to_all(z_sum(rest, ups, downs, up2, down2), ("y", "c"), 0, 0, tiled=True)
    spread, combined = combine(place, gate, grad, returned)
    gate_parts = lax.all_to_all(spread, ("x", "z"), 0, 0, tiled=True)
    hidden_grad, weight_grad, scale_grad = backward(where, *weights, packs)
    gate_parts, hidden_grad = lax.optimization_barrier((gate_parts, hidden_grad))
    gate_grad = gate_sum(gate_parts)
    return combined.T, gate_grad.T, hidden_grad[None], weight_grad[None], scale_grad.reshape(group_scales.shape)


def solution(mesh):
    fine = Mesh(mesh.devices.reshape(NY, NC, NX, NZ), ("y", "c", "x", "z"))
    expert, dp = ("y", "c"), ("x", "z")
    return jax.shard_map(
        on_device,
        mesh=fine,
        in_specs=(
            P(expert, dp, None),
            P(expert, dp, None),
            P(expert, dp, None),
            P(expert, None),
            P(expert, None),
            P(expert, dp),
        ),
        out_specs=(
            P(expert, dp),
            P(expert, None),
            P(expert, dp, None),
            P(expert, dp, None),
            P(expert, dp, None),
        ),
        check_vma=False,
    )
```

```python
import jax
import jax.numpy as jnp
from jax import lax
from jax.experimental import pallas as pl
from jax.experimental.pallas import tpu as pltpu
from jax.sharding import Mesh, PartitionSpec as P

EXPERTS = 8
GROUP = 32
CAP = 128
NY, NC, NX, NZ = 4, 2, 4, 8
COLS = 64
SLOTS = EXPERTS * CAP
BLOCK = NZ * COLS
SMALL = pltpu.CompilerParams(vmem_limit_bytes=16 * 1024 * 1024)
LARGE = pltpu.CompilerParams(vmem_limit_bytes=32 * 1024 * 1024)
F32, BF16, I32 = jnp.float32, jnp.bfloat16, jnp.int32


sds = jax.ShapeDtypeStruct
HBM, VMEM, SMEM = (pl.BlockSpec(memory_space=m) for m in (pltpu.HBM, pltpu.VMEM, pltpu.SMEM))


def near(array):
    return pltpu.with_memory_space_constraint(array, pltpu.VMEM)


def away(array):
    return pltpu.with_memory_space_constraint(array, pltpu.HBM)


def call(body, name, where, operands, outs, scratch=(), far=(), keep=None):
    heads = [] if where is None else [where]
    keep = len(outs) if keep is None else keep
    return pl.pallas_call(
        body,
        in_specs=[SMEM] * len(heads) + [HBM] * len(far) + [VMEM] * len(operands),
        out_specs=[VMEM] * len(outs),
        out_shape=[(pltpu.VMEM if i < keep else sds)(*out) for i, out in enumerate(outs)],
        scratch_shapes=list(scratch),
        compiler_params=SMALL,
        name=name,
    )(*heads, *[away(a) for a in far], *[near(a) for a in operands])


def dequant(codes_ref, scales_ref, tile, table_ref):
    units, width = codes_ref.shape
    tiles = scales_ref.shape[0] // (units // GROUP)
    for j in range(width // 128):
        lanes = slice(j * 128, (j + 1) * 128)
        for g in range(units // GROUP):
            rows = slice(g * GROUP, (g + 1) * GROUP)
            scale = scales_ref[pl.ds(g * tiles + tile + j, 1), :]
            table_ref[rows, lanes] = (codes_ref[rows, lanes].astype(F32) * scale).astype(BF16)


def picker(place_ref, k):
    slots = lax.broadcasted_iota(I32, (SLOTS, place_ref.shape[1]), 0)
    return (place_ref[k : k + 1, :] == slots).astype(BF16)


def slot_body(index_ref, gate_ref, grad_ref, place_ref, out_ref):
    tokens = index_ref.shape[1]
    experts = lax.broadcasted_iota(I32, (EXPERTS, tokens), 0)
    hot = [(index_ref[k : k + 1, :] == experts).astype(F32) for k in range(2)]
    row = lax.broadcasted_iota(I32, (tokens, tokens), 0)
    col = lax.broadcasted_iota(I32, (tokens, tokens), 1)
    before = (row < col).astype(BF16)
    counts = jnp.dot((hot[0] + hot[1]).astype(BF16), before, preferred_element_type=F32)
    for k in range(2):
        rank = jnp.sum(counts * hot[k], axis=0, keepdims=True).astype(I32)
        place_ref[k : k + 1, :] = jnp.where(rank < CAP, index_ref[k : k + 1, :] * CAP + rank, -1)
    grad = grad_ref[...].astype(F32)
    total = None
    for k in range(2):
        value = (gate_ref[k : k + 1, :] * grad).astype(BF16)
        piece = lax.dot_general(
            value, picker(place_ref, k), (((1,), (1,)), ((), ())), preferred_element_type=F32
        )
        total = piece if total is None else total + piece
    total = total.astype(BF16)
    for e in range(EXPERTS):
        out_ref[e] = total[:, e * CAP : (e + 1) * CAP]


def slot_grads(index, gate, grad):
    outs = [(index.shape, I32), ((EXPERTS, COLS, CAP), BF16)]
    return call(slot_body, "slot_grads", None, [index, gate, grad], outs)


def loads(where_ref, hops, hidden_hbm, codes_hbm, scales_hbm, hidden, codes, scales, sems):
    copies = [
        pltpu.make_async_copy(scales_hbm, scales, sems.at[0]),
        pltpu.make_async_copy(hidden_hbm, hidden, sems.at[1]),
    ]
    for i, hop in enumerate(hops):
        start = pl.multiple_of(lax.rem(where_ref[0] + hop, NX) * BLOCK, BLOCK)
        copies.append(pltpu.make_async_copy(codes_hbm.at[:, pl.ds(start, BLOCK)], codes.at[i], sems.at[2 + i]))
    for copy in copies:
        copy.start()
    copies[0].wait()
    return copies[1:]


def buffers(units, count):
    return [
        pltpu.VMEM((units, SLOTS), BF16),
        pltpu.VMEM((count, units, BLOCK), I32),
        pltpu.VMEM((units // GROUP * (NX * BLOCK // 128), 128), F32),
        pltpu.VMEM((units, BLOCK), BF16),
        pltpu.SemaphoreType.DMA((2 + count,)),
    ]


def block_value(where_ref, hops, hidden, codes, scales, table, copy, others=()):
    copy.wait()
    dequant(codes, scales, lax.rem(where_ref[0] + hops, NX) * (BLOCK // 128), table)
    for other in others:
        other.wait()
    return lax.dot_general(table[...], hidden[...], (((0,), (0,)), ((), ())), preferred_element_type=F32)


def far_body(where_ref, hidden_hbm, codes_hbm, scales_hbm, top_ref, bottom_ref, hidden, codes, scales, table, sems):
    first, *copies = loads(where_ref, (2,), hidden_hbm, codes_hbm, scales_hbm, hidden, codes, scales, sems)
    value = block_value(where_ref, 2, hidden, codes.at[0], scales, table, copies[0], (first,)).astype(BF16)
    top_ref[...] = value[: BLOCK // 2]
    bottom_ref[...] = value[BLOCK // 2 :]


def forward_far(where, *arrays):
    half = ((BLOCK // 2, SLOTS), BF16)
    return call(far_body, "forward_far", where, [], [half, half], buffers(arrays[0].shape[0], 1), arrays)


def join_body(
    where_ref, hidden_hbm, codes_hbm, scales_hbm, top_ref, bottom_ref, up_ref, down_ref, own_ref, hidden, codes, scales, table, sems
):
    first, *copies = loads(where_ref, (1, 3, 0), hidden_hbm, codes_hbm, scales_hbm, hidden, codes, scales, sems)
    half = BLOCK // 2
    value = block_value(where_ref, 1, hidden, codes.at[0], scales, table, copies[0], (first,))
    up_ref[:half] = (value[:half] + top_ref[...].astype(F32)).astype(BF16)
    up_ref[half:] = value[half:].astype(BF16)
    value = block_value(where_ref, 3, hidden, codes.at[1], scales, table, copies[1])
    down_ref[:half] = value[:half].astype(BF16)
    down_ref[half:] = (value[half:] + bottom_ref[...].astype(F32)).astype(BF16)
    own_ref[...] = block_value(where_ref, 0, hidden, codes.at[2], scales, table, copies[2])


def forward_join(where, hidden, codes, scales, top, bottom):
    outs = [((BLOCK, SLOTS), BF16)] * 2 + [((BLOCK, SLOTS), F32)]
    far = (hidden, codes, scales)
    return call(join_body, "forward_join", where, [top, bottom], outs, buffers(hidden.shape[0], 3), far)


def x_sum_body(where_ref, own_ref, up_ref, down_ref, ups_ref, downs_ref, far_ref, up2_ref, down2_ref, rest_ref):
    def total(hops):
        rows = pl.ds(pl.multiple_of(lax.rem(where_ref[1] + hops, NZ) * COLS, COLS), COLS)
        return own_ref[rows, :] + up_ref[rows, :].astype(F32) + down_ref[rows, :].astype(F32)

    ups_ref[0] = total(3).astype(BF16)
    ups_ref[1] = total(1).astype(BF16)
    downs_ref[0] = total(5).astype(BF16)
    downs_ref[1] = total(7).astype(BF16)
    far_ref[...] = total(4).astype(BF16)
    up2_ref[...] = total(2)
    down2_ref[...] = total(6)
    rest_ref[...] = total(0)


def x_sum(where, *arrays):
    one, two = (COLS, SLOTS), (2, COLS, SLOTS)
    outs = [(two, BF16), (two, BF16), (one, BF16), (one, F32), (one, F32), (one, F32)]
    return call(x_sum_body, "x_sum", where, arrays, outs)


def mid_sum_body(up2_ref, down2_ref, ups_ref, downs_ref, far_ref, up_out, down_out):
    up_out[...] = (up2_ref[...] + ups_ref[0].astype(F32) + far_ref[...].astype(F32)).astype(BF16)
    down_out[...] = (down2_ref[...] + downs_ref[0].astype(F32)).astype(BF16)


def mid_sum(*arrays):
    return call(mid_sum_body, "mid_sum", None, arrays, [((COLS, SLOTS), BF16)] * 2)


def z_sum_body(rest_ref, ups_ref, downs_ref, up_ref, down_ref, out_ref):
    total = rest_ref[...] + ups_ref[1].astype(F32) + downs_ref[1].astype(F32)
    total = (total + up_ref[...].astype(F32) + down_ref[...].astype(F32)).astype(BF16)
    for g in range(EXPERTS):
        out_ref[g] = total[:, g * CAP : (g + 1) * CAP]


def z_sum(*arrays):
    return call(z_sum_body, "z_sum", None, arrays, [((EXPERTS, COLS, CAP), BF16)])[0]


def combine_body(place_ref, gate_ref, grad_ref, back_ref, spread_ref, out_ref):
    back = jnp.concatenate([back_ref[e] for e in range(EXPERTS)], axis=1)
    grad = grad_ref[...].astype(F32)
    total = None
    for k in range(2):
        got = jnp.dot(back, picker(place_ref, k), preferred_element_type=F32)
        piece = gate_ref[k : k + 1, :] * got
        total = piece if total is None else total + piece
        part = jnp.sum(grad * got, axis=0, keepdims=True)
        for j in range(4):
            line = part[:, j * 128 : (j + 1) * 128]
            spread_ref[:, k * 4 + j : k * 4 + j + 1, :] = jnp.broadcast_to(line[None], (NX * NZ, 1, 128))
    out_ref[...] = total.astype(BF16)


def combine(place, gate, grad, back):
    outs = [((NX * NZ, 8, 128), F32), (grad.shape, BF16)]
    return call(combine_body, "combine", None, [place, gate, grad, back], outs, keep=1)


def gate_sum_body(parts_ref, out_ref):
    total = jnp.sum(parts_ref[...], axis=0)
    for k in range(2):
        for j in range(4):
            out_ref[k : k + 1, j * 128 : (j + 1) * 128] = total[k * 4 + j : k * 4 + j + 1, :]


def gate_sum(parts):
    return call(gate_sum_body, "gate_sum", None, [parts], [((2, 512), F32)], keep=0)[0]


ORDER = (0, 3, 5, 4, 1, 7, 2, 6)
EARLY = 6


def pack_body(*refs):
    for i in range(EARLY):
        refs[-1][i] = refs[i][...]


def pack(*pieces):
    return call(pack_body, "pack", None, pieces, [((EARLY, EXPERTS, COLS, CAP), BF16)])[0]


def pack_all_body(first_ref, *refs):
    second_ref, all_ref = refs[-2:]
    all_ref[:EARLY] = first_ref[...]
    for i in range(NZ - EARLY):
        second_ref[i] = refs[i][...]
        all_ref[EARLY + i] = refs[i][...]


def pack_all(*pieces):
    outs = [((count, EXPERTS, COLS, CAP), BF16) for count in (NZ - EARLY, NZ)]
    return call(pack_all_body, "pack_all", None, pieces, outs)


SIDES = (0, 1, 3, 2)


def backward(where, hidden, codes, scales, packs):
    units, slots = hidden.shape
    features = codes.shape[1]
    count, tiles = NX, BLOCK // 128
    operands = [hidden, codes, scales, *packs]

    def body(where_ref, hidden_hbm, codes_hbm, scales_hbm, *rest):
        packs_hbm, rest = rest[: len(packs)], rest[len(packs) :]
        hidden_out, weight_out, scale_out, hidden_v, codes_v, scales_v, grads, table, weight, sems = rest
        x_of = [lax.rem(where_ref[0] + side, NX) for side in SIDES]
        lanes_of = [pl.ds(pl.multiple_of(x * BLOCK, BLOCK), BLOCK) for x in x_of]
        head = [
            pltpu.make_async_copy(hidden_hbm, hidden_v, sems.at[0]),
            pltpu.make_async_copy(scales_hbm, scales_v, sems.at[1]),
        ]
        parts, arrive = [], []
        for n in range(count):
            parts.append(pltpu.make_async_copy(codes_hbm.at[:, lanes_of[n]], codes_v.at[n], sems.at[8 + n]))
            arrive.append([])
            for k in range(NZ):
                z = lax.rem(where_ref[1] + ORDER[k], NZ)
                rows = pl.ds(pl.multiple_of(n * BLOCK + z * COLS, COLS), COLS)
                half, place = (0, k) if k < EARLY else (1, k - EARLY)
                source = packs_hbm[(0, 1 + half, 3 + half, 5)[n]].at[k if n in (0, NX - 1) else place]
                sem = sems.at[8 + count + n * NZ + k]
                arrive[n].append(pltpu.make_async_copy(source, grads.at[:, rows], sem))
        head[0].start()
        for copy in arrive[0]:
            copy.start()
        for copy in head[1:]:
            copy.start()
        parts[0].start()
        for n in range(1, count):
            for copy in arrive[n]:
                copy.start()
            parts[n].start()
        for copy in head:
            copy.wait()
        copies = []
        for n in range(count):
            rows_here = slice(n * BLOCK, (n + 1) * BLOCK)
            for copy in arrive[n]:
                copy.wait()
            block = jnp.concatenate([grads[g, rows_here, :] for g in range(EXPERTS)], axis=1)
            weight[n] = lax.dot_general(
                hidden_v[...], block, (((1,), (1,)), ((), ())), preferred_element_type=F32
            )
            copies.append(pltpu.make_async_copy(weight.at[n], weight_out.at[:, lanes_of[n]], sems.at[4 + n]))
            copies[n].start()
            parts[n].wait()
            dequant(codes_v.at[n], scales_v, x_of[n] * tiles, table.at[:, rows_here])
            for g in range(units // GROUP):
                rows = slice(g * GROUP, (g + 1) * GROUP)
                line = jnp.sum(weight[n, rows, :] * codes_v[n, rows, :].astype(F32), axis=0, keepdims=True)
                for j in range(tiles):
                    row = (g * NX + x_of[n]) * tiles + j
                    scale_out[pl.ds(row, 1), :] = line[:, j * 128 : (j + 1) * 128]
        block = jnp.concatenate([grads[g] for g in range(EXPERTS)], axis=1)
        hidden_out[...] = jnp.dot(table[...], block, preferred_element_type=F32).astype(BF16)
        for copy in copies:
            copy.wait()

    return pl.pallas_call(
        body,
        in_specs=[SMEM] + [HBM] * len(operands),
        out_specs=[VMEM, HBM, VMEM],
        out_shape=[sds((units, slots), BF16), sds((units, features), F32), sds(scales.shape, F32)],
        scratch_shapes=[
            pltpu.VMEM((units, slots), BF16),
            pltpu.VMEM((count, units, BLOCK), I32),
            pltpu.VMEM(scales.shape, F32),
            pltpu.VMEM((EXPERTS, count * BLOCK, CAP), BF16),
            pltpu.VMEM((units, count * BLOCK), BF16),
            pltpu.VMEM((count, units, BLOCK), F32),
            pltpu.SemaphoreType.DMA((8 + count + count * NZ,)),
        ],
        compiler_params=LARGE,
        name="backward",
    )(where, *[away(a) for a in operands])


def shift(value, axis, by):
    size = NX if axis == "x" else NZ
    return lax.ppermute(value, axis, [(i, (i + by) % size) for i in range(size)])


def on_device(hidden, weight_codes, group_scales, expert_index, gate_values, output_grad):
    weights = (hidden[0], weight_codes[0], group_scales.reshape(-1, 128))
    index, gate, grad = expert_index.T, gate_values.T, output_grad.T
    where = jnp.stack([lax.axis_index("x"), lax.axis_index("z")]).astype(I32)

    far_top, far_bottom = forward_far(where, *weights)
    far_top = shift(far_top, "x", 1)
    far_bottom = shift(far_bottom, "x", -1)

    place, outbound = slot_grads(index, gate, grad)
    shard = lax.all_to_all(outbound, ("y", "c"), 0, 0, tiled=True)
    far_top, far_bottom, shard = lax.optimization_barrier((far_top, far_bottom, shard))
    up, down, own = forward_join(where, *weights, far_top, far_bottom)
    up, down, shard = lax.optimization_barrier((up, down, shard))
    up = shift(up, "x", 1)
    down = shift(down, "x", -1)
    along = {k: shift(shard, "z", -k) for k in ORDER[1:]}
    up, down, *early = lax.optimization_barrier((up, down, *[along[k] for k in ORDER[1:EARLY]]))
    half = pack(shard, *early)
    packs = [shift(half, "x", -1), shift(half, "x", 1)]

    ups, downs, far, up2, down2, rest = x_sum(where, own, up, down)
    rest, *late = lax.optimization_barrier((rest, *[along[k] for k in ORDER[EARLY:]]))
    other, mine = pack_all(half, *late)
    ups, downs, far = shift(ups, "z", 1), shift(downs, "z", -1), shift(far, "z", 2)
    up2, down2 = mid_sum(up2, down2, ups, downs, far)
    up2, down2, mine = lax.optimization_barrier((up2, down2, mine))
    opposite = shift(mine, "x", 2)
    up2, down2 = shift(up2, "z", 2), shift(down2, "z", -2)
    up2, down2, other, *packs = lax.optimization_barrier((up2, down2, other, *packs))
    packs = [mine, packs[0], shift(other, "x", -1), packs[1], shift(other, "x", 1), opposite]
    returned = lax.all_to_all(z_sum(rest, ups, downs, up2, down2), ("y", "c"), 0, 0, tiled=True)
    returned, packs[2], packs[4] = lax.optimization_barrier((returned, packs[2], packs[4]))
    spread, combined = combine(place, gate, grad, returned)
    gate_parts = lax.all_to_all(spread, ("x", "z"), 0, 0, tiled=True)
    hidden_grad, weight_grad, scale_grad = backward(where, *weights, packs)
    gate_parts, hidden_grad = lax.optimization_barrier((gate_parts, hidden_grad))
    gate_grad = gate_sum(gate_parts)
    return combined.T, gate_grad.T, hidden_grad[None], weight_grad[None], scale_grad.reshape(group_scales.shape)


def solution(mesh):
    fine = Mesh(mesh.devices.reshape(NY, NC, NX, NZ), ("y", "c", "x", "z"))
    expert, dp = ("y", "c"), ("x", "z")
    return jax.shard_map(
        on_device,
        mesh=fine,
        in_specs=(
            P(expert, dp, None),
            P(expert, dp, None),
            P(expert, dp, None),
            P(expert, None),
            P(expert, None),
            P(expert, dp),
        ),
        out_specs=(
            P(expert, dp),
            P(expert, None),
            P(expert, dp, None),
            P(expert, dp, None),
            P(expert, dp, None),
        ),
        check_vma=False,
    )
```

```python
import jax
import jax.numpy as jnp
from jax import lax
from jax.experimental import pallas as pl
from jax.experimental.pallas import tpu as pltpu
from jax.sharding import Mesh, PartitionSpec as P

EXPERTS = 8
GROUP = 32
CAP = 128
NY, NC, NX, NZ = 4, 2, 4, 8
COLS = 64
SLOTS = EXPERTS * CAP
BLOCK = NZ * COLS
SMALL = pltpu.CompilerParams(vmem_limit_bytes=16 * 1024 * 1024)
LARGE = pltpu.CompilerParams(vmem_limit_bytes=32 * 1024 * 1024)
F32, BF16, I32 = jnp.float32, jnp.bfloat16, jnp.int32


sds = jax.ShapeDtypeStruct
HBM, VMEM, SMEM = (pl.BlockSpec(memory_space=m) for m in (pltpu.HBM, pltpu.VMEM, pltpu.SMEM))


def near(array):
    return pltpu.with_memory_space_constraint(array, pltpu.VMEM)


def away(array):
    return pltpu.with_memory_space_constraint(array, pltpu.HBM)


def call(body, name, where, operands, outs, scratch=(), far=(), keep=None):
    heads = [] if where is None else [where]
    keep = len(outs) if keep is None else keep
    return pl.pallas_call(
        body,
        in_specs=[SMEM] * len(heads) + [HBM] * len(far) + [VMEM] * len(operands),
        out_specs=[VMEM] * len(outs),
        out_shape=[(pltpu.VMEM if i < keep else sds)(*out) for i, out in enumerate(outs)],
        scratch_shapes=list(scratch),
        compiler_params=SMALL,
        name=name,
    )(*heads, *[away(a) for a in far], *[near(a) for a in operands])


def dequant(codes_ref, scales_ref, tile, table_ref):
    units, width = codes_ref.shape
    tiles = scales_ref.shape[0] // (units // GROUP)
    for j in range(width // 128):
        lanes = slice(j * 128, (j + 1) * 128)
        for g in range(units // GROUP):
            rows = slice(g * GROUP, (g + 1) * GROUP)
            scale = scales_ref[pl.ds(g * tiles + tile + j, 1), :]
            table_ref[rows, lanes] = (codes_ref[rows, lanes].astype(F32) * scale).astype(BF16)


def picker(place_ref, k):
    slots = lax.broadcasted_iota(I32, (SLOTS, place_ref.shape[1]), 0)
    return (place_ref[k : k + 1, :] == slots).astype(BF16)


def slot_body(index_ref, gate_ref, grad_ref, place_ref, out_ref):
    tokens = index_ref.shape[1]
    experts = lax.broadcasted_iota(I32, (EXPERTS, tokens), 0)
    hot = [(index_ref[k : k + 1, :] == experts).astype(F32) for k in range(2)]
    row = lax.broadcasted_iota(I32, (tokens, tokens), 0)
    col = lax.broadcasted_iota(I32, (tokens, tokens), 1)
    before = (row < col).astype(BF16)
    counts = jnp.dot((hot[0] + hot[1]).astype(BF16), before, preferred_element_type=F32)
    for k in range(2):
        rank = jnp.sum(counts * hot[k], axis=0, keepdims=True).astype(I32)
        place_ref[k : k + 1, :] = jnp.where(rank < CAP, index_ref[k : k + 1, :] * CAP + rank, -1)
    grad = grad_ref[...].astype(F32)
    total = None
    for k in range(2):
        value = (gate_ref[k : k + 1, :] * grad).astype(BF16)
        piece = lax.dot_general(
            value, picker(place_ref, k), (((1,), (1,)), ((), ())), preferred_element_type=F32
        )
        total = piece if total is None else total + piece
    total = total.astype(BF16)
    for e in range(EXPERTS):
        out_ref[e] = total[:, e * CAP : (e + 1) * CAP]


def slot_grads(index, gate, grad):
    outs = [(index.shape, I32), ((EXPERTS, COLS, CAP), BF16)]
    return call(slot_body, "slot_grads", None, [index, gate, grad], outs)


def loads(where_ref, hops, hidden_hbm, codes_hbm, scales_hbm, hidden, codes, scales, sems):
    copies = [
        pltpu.make_async_copy(scales_hbm, scales, sems.at[0]),
        pltpu.make_async_copy(hidden_hbm, hidden, sems.at[1]),
    ]
    for i, hop in enumerate(hops):
        start = pl.multiple_of(lax.rem(where_ref[0] + hop, NX) * BLOCK, BLOCK)
        copies.append(pltpu.make_async_copy(codes_hbm.at[:, pl.ds(start, BLOCK)], codes.at[i], sems.at[2 + i]))
    for copy in copies:
        copy.start()
    copies[0].wait()
    return copies[1:]


def buffers(units, count):
    return [
        pltpu.VMEM((units, SLOTS), BF16),
        pltpu.VMEM((count, units, BLOCK), I32),
        pltpu.VMEM((units // GROUP * (NX * BLOCK // 128), 128), F32),
        pltpu.VMEM((units, BLOCK), BF16),
        pltpu.SemaphoreType.DMA((2 + count,)),
    ]


def block_value(where_ref, hops, hidden, codes, scales, table, copy, others=()):
    copy.wait()
    dequant(codes, scales, lax.rem(where_ref[0] + hops, NX) * (BLOCK // 128), table)
    for other in others:
        other.wait()
    return lax.dot_general(table[...], hidden[...], (((0,), (0,)), ((), ())), preferred_element_type=F32)


def far_body(where_ref, hidden_hbm, codes_hbm, scales_hbm, top_ref, bottom_ref, hidden, codes, scales, table, sems):
    first, *copies = loads(where_ref, (2,), hidden_hbm, codes_hbm, scales_hbm, hidden, codes, scales, sems)
    value = block_value(where_ref, 2, hidden, codes.at[0], scales, table, copies[0], (first,)).astype(BF16)
    top_ref[...] = value[: BLOCK // 2]
    bottom_ref[...] = value[BLOCK // 2 :]


def forward_far(where, *arrays):
    half = ((BLOCK // 2, SLOTS), BF16)
    return call(far_body, "forward_far", where, [], [half, half], buffers(arrays[0].shape[0], 1), arrays)


def join_body(
    where_ref, hidden_hbm, codes_hbm, scales_hbm, top_ref, bottom_ref, up_ref, down_ref, own_ref, hidden, codes, scales, table, sems
):
    first, *copies = loads(where_ref, (1, 3, 0), hidden_hbm, codes_hbm, scales_hbm, hidden, codes, scales, sems)
    half = BLOCK // 2
    value = block_value(where_ref, 1, hidden, codes.at[0], scales, table, copies[0], (first,))
    up_ref[:half] = (value[:half] + top_ref[...].astype(F32)).astype(BF16)
    up_ref[half:] = value[half:].astype(BF16)
    value = block_value(where_ref, 3, hidden, codes.at[1], scales, table, copies[1])
    down_ref[:half] = value[:half].astype(BF16)
    down_ref[half:] = (value[half:] + bottom_ref[...].astype(F32)).astype(BF16)
    own_ref[...] = block_value(where_ref, 0, hidden, codes.at[2], scales, table, copies[2])


def forward_join(where, hidden, codes, scales, top, bottom):
    outs = [((BLOCK, SLOTS), BF16)] * 2 + [((BLOCK, SLOTS), F32)]
    far = (hidden, codes, scales)
    return call(join_body, "forward_join", where, [top, bottom], outs, buffers(hidden.shape[0], 3), far)


def x_sum_body(where_ref, own_ref, up_ref, down_ref, ups_ref, downs_ref, far_ref, up2_ref, down2_ref, rest_ref):
    def total(hops):
        rows = pl.ds(pl.multiple_of(lax.rem(where_ref[1] + hops, NZ) * COLS, COLS), COLS)
        return own_ref[rows, :] + up_ref[rows, :].astype(F32) + down_ref[rows, :].astype(F32)

    ups_ref[0] = total(3).astype(BF16)
    ups_ref[1] = total(1).astype(BF16)
    downs_ref[0] = total(5).astype(BF16)
    downs_ref[1] = total(7).astype(BF16)
    far_ref[...] = total(4).astype(BF16)
    up2_ref[...] = total(2)
    down2_ref[...] = total(6)
    rest_ref[...] = total(0)


def x_sum(where, *arrays):
    one, two = (COLS, SLOTS), (2, COLS, SLOTS)
    outs = [(two, BF16), (two, BF16), (one, BF16), (one, F32), (one, F32), (one, F32)]
    return call(x_sum_body, "x_sum", where, arrays, outs)


def mid_sum_body(up2_ref, down2_ref, ups_ref, downs_ref, far_ref, up_out, down_out):
    up_out[...] = (up2_ref[...] + ups_ref[0].astype(F32) + far_ref[...].astype(F32)).astype(BF16)
    down_out[...] = (down2_ref[...] + downs_ref[0].astype(F32)).astype(BF16)


def mid_sum(*arrays):
    return call(mid_sum_body, "mid_sum", None, arrays, [((COLS, SLOTS), BF16)] * 2)


def z_sum_body(rest_ref, ups_ref, downs_ref, up_ref, down_ref, out_ref):
    total = rest_ref[...] + ups_ref[1].astype(F32) + downs_ref[1].astype(F32)
    total = (total + up_ref[...].astype(F32) + down_ref[...].astype(F32)).astype(BF16)
    for g in range(EXPERTS):
        out_ref[g] = total[:, g * CAP : (g + 1) * CAP]


def z_sum(*arrays):
    return call(z_sum_body, "z_sum", None, arrays, [((EXPERTS, COLS, CAP), BF16)])[0]


def combine_body(place_ref, gate_ref, grad_ref, back_ref, spread_ref, out_ref):
    back = jnp.concatenate([back_ref[e] for e in range(EXPERTS)], axis=1)
    grad = grad_ref[...].astype(F32)
    total = None
    for k in range(2):
        got = jnp.dot(back, picker(place_ref, k), preferred_element_type=F32)
        piece = gate_ref[k : k + 1, :] * got
        total = piece if total is None else total + piece
        part = jnp.sum(grad * got, axis=0, keepdims=True)
        for j in range(4):
            line = part[:, j * 128 : (j + 1) * 128]
            spread_ref[:, k * 4 + j : k * 4 + j + 1, :] = jnp.broadcast_to(line[None], (NX * NZ, 1, 128))
    out_ref[...] = total.astype(BF16)


def combine(place, gate, grad, back):
    outs = [((NX * NZ, 8, 128), F32), (grad.shape, BF16)]
    return call(combine_body, "combine", None, [place, gate, grad, back], outs, keep=1)


def gate_sum_body(parts_ref, out_ref):
    total = jnp.sum(parts_ref[...], axis=0)
    for k in range(2):
        for j in range(4):
            out_ref[k : k + 1, j * 128 : (j + 1) * 128] = total[k * 4 + j : k * 4 + j + 1, :]


def gate_sum(parts):
    return call(gate_sum_body, "gate_sum", None, [parts], [((2, 512), F32)], keep=0)[0]


NEAREST = (0, 1, 7, 2, 6, 3, 5, 4)


def pack_body(*refs):
    for i, k in enumerate(NEAREST):
        refs[-1][k] = refs[i][...]


def pack(*pieces):
    return call(pack_body, "pack", None, pieces, [((NZ, EXPERTS, COLS, CAP), BF16)])[0]


SIDES = (0, 1, 3, 2)


def backward_body(where_ref, hidden_hbm, codes_hbm, scales_hbm, *rest):
    packs = rest[: NX + 1]
    hidden_out, weight_out, scale_out = rest[NX + 1 : NX + 4]
    hidden, codes, scales, grads, table, weight, sems = rest[NX + 4 :]
    units = hidden.shape[0]
    tiles = BLOCK // 128
    x_of = [lax.rem(where_ref[0] + side, NX) for side in SIDES]
    lanes_of = [pl.ds(pl.multiple_of(x * BLOCK, BLOCK), BLOCK) for x in x_of]
    head = [
        pltpu.make_async_copy(hidden_hbm, hidden, sems.at[0]),
        pltpu.make_async_copy(scales_hbm, scales, sems.at[1]),
    ]
    parts, arrive = [], []
    for n in range(NX):
        parts.append(pltpu.make_async_copy(codes_hbm.at[:, lanes_of[n]], codes.at[n], sems.at[2 + n]))
        arrive.append([])
        for k in range(NZ):
            z = lax.rem(where_ref[1] + k, NZ)
            rows = pl.ds(pl.multiple_of(n * BLOCK + z * COLS, COLS), COLS)
            source = packs[n].at[k] if n < NX - 1 else packs[n + k // 4].at[k % 4]
            arrive[n].append(pltpu.make_async_copy(source, grads.at[:, rows], sems.at[8 + n * NZ + k]))
    head[0].start()
    for copy in arrive[0]:
        copy.start()
    head[1].start()
    parts[0].start()
    for n in range(1, NX):
        for copy in arrive[n]:
            copy.start()
        parts[n].start()
    head[0].wait()
    head[1].wait()
    copies = []
    for n in range(NX):
        rows_here = slice(n * BLOCK, (n + 1) * BLOCK)
        for copy in arrive[n]:
            copy.wait()
        block = jnp.concatenate([grads[g, rows_here, :] for g in range(EXPERTS)], axis=1)
        slot = n % 2
        if n >= 2:
            copies[n - 2].wait()
        weight[slot] = lax.dot_general(
            hidden[...], block, (((1,), (1,)), ((), ())), preferred_element_type=F32
        )
        copies.append(pltpu.make_async_copy(weight.at[slot], weight_out.at[:, lanes_of[n]], sems.at[6 + slot]))
        copies[n].start()
        parts[n].wait()
        dequant(codes.at[n], scales, x_of[n] * tiles, table.at[:, rows_here])
        for g in range(units // GROUP):
            rows = slice(g * GROUP, (g + 1) * GROUP)
            line = jnp.sum(weight[slot, rows, :] * codes[n, rows, :].astype(F32), axis=0, keepdims=True)
            for j in range(tiles):
                row = (g * NX + x_of[n]) * tiles + j
                scale_out[pl.ds(row, 1), :] = line[:, j * 128 : (j + 1) * 128]
    block = jnp.concatenate([grads[g] for g in range(EXPERTS)], axis=1)
    hidden_out[...] = jnp.dot(table[...], block, preferred_element_type=F32).astype(BF16)
    copies[2].wait()
    copies[3].wait()


def backward(where, hidden, codes, scales, packs):
    units, slots = hidden.shape
    features = codes.shape[1]
    return pl.pallas_call(
        backward_body,
        in_specs=[SMEM] + [HBM] * (4 + NX),
        out_specs=[VMEM, HBM, VMEM],
        out_shape=[sds((units, slots), BF16), sds((units, features), F32), sds(scales.shape, F32)],
        scratch_shapes=[
            pltpu.VMEM((units, slots), BF16),
            pltpu.VMEM((NX, units, BLOCK), I32),
            pltpu.VMEM(scales.shape, F32),
            pltpu.VMEM((EXPERTS, features, CAP), BF16),
            pltpu.VMEM((units, features), BF16),
            pltpu.VMEM((2, units, BLOCK), F32),
            pltpu.SemaphoreType.DMA((8 + NX * NZ,)),
        ],
        compiler_params=LARGE,
        name="backward",
    )(where, *[away(a) for a in (hidden, codes, scales, *packs)])


def shift(value, axis, by):
    size = NX if axis == "x" else NZ
    return lax.ppermute(value, axis, [(i, (i + by) % size) for i in range(size)])


def on_device(hidden, weight_codes, group_scales, expert_index, gate_values, output_grad):
    weights = (hidden[0], weight_codes[0], group_scales.reshape(-1, 128))
    index, gate, grad = expert_index.T, gate_values.T, output_grad.T
    where = jnp.stack([lax.axis_index("x"), lax.axis_index("z")]).astype(I32)

    far_top, far_bottom = forward_far(where, *weights)
    far_top = shift(far_top, "x", 1)
    far_bottom = shift(far_bottom, "x", -1)

    place, outbound = slot_grads(index, gate, grad)
    shard = lax.all_to_all(outbound, ("y", "c"), 0, 0, tiled=True)
    far_top, far_bottom, shard = lax.optimization_barrier((far_top, far_bottom, shard))
    up, down, own = forward_join(where, *weights, far_top, far_bottom)
    up, down, shard = lax.optimization_barrier((up, down, shard))
    up = shift(up, "x", 1)
    down = shift(down, "x", -1)
    along = [shift(shard, "z", -k) for k in NEAREST[1:]]
    up, down, *along[3:] = lax.optimization_barrier((up, down, *along[3:]))

    ups, downs, far, up2, down2, rest = x_sum(where, own, up, down)
    rest, *along = lax.optimization_barrier((rest, *along))
    mine = pack(shard, *along)
    packs = [mine, shift(mine, "x", -1), shift(mine, "x", 1)]
    ups, downs, far, _ = lax.optimization_barrier((ups, downs, far, mine))
    ups, downs, far = shift(ups, "z", 1), shift(downs, "z", -1), shift(far, "z", 2)
    up2, down2 = mid_sum(up2, down2, ups, downs, far)
    up2, down2 = shift(up2, "z", 2), shift(down2, "z", -2)
    up2, down2, packs[1], packs[2] = lax.optimization_barrier((up2, down2, packs[1], packs[2]))
    packs += [shift(packs[1][: NZ // 2], "x", -1), shift(packs[2][NZ // 2 :], "x", 1)]
    returned = lax.all_to_all(z_sum(rest, ups, downs, up2, down2), ("y", "c"), 0, 0, tiled=True)
    spread, combined = combine(place, gate, grad, returned)
    gate_parts = lax.all_to_all(spread, ("x", "z"), 0, 0, tiled=True)
    hidden_grad, weight_grad, scale_grad = backward(where, *weights, packs)
    gate_parts, hidden_grad = lax.optimization_barrier((gate_parts, hidden_grad))
    gate_grad = gate_sum(gate_parts)
    return combined.T, gate_grad.T, hidden_grad[None], weight_grad[None], scale_grad.reshape(group_scales.shape)


def solution(mesh):
    fine = Mesh(mesh.devices.reshape(NY, NC, NX, NZ), ("y", "c", "x", "z"))
    expert, dp = ("y", "c"), ("x", "z")
    return jax.shard_map(
        on_device,
        mesh=fine,
        in_specs=(
            P(expert, dp, None),
            P(expert, dp, None),
            P(expert, dp, None),
            P(expert, None),
            P(expert, None),
            P(expert, dp),
        ),
        out_specs=(
            P(expert, dp),
            P(expert, None),
            P(expert, dp, None),
            P(expert, dp, None),
            P(expert, dp, None),
        ),
        check_vma=False,
    )
```

```python
import jax
import jax.numpy as jnp
from jax import lax
from jax.experimental import pallas as pl
from jax.experimental.pallas import tpu as pltpu
from jax.sharding import Mesh, PartitionSpec as P

EXPERTS = 8
GROUP = 32
CAP = 128
NY, NC, NX, NZ = 4, 2, 4, 8
COLS = 64
SLOTS = EXPERTS * CAP
BLOCK = NZ * COLS
SMALL = pltpu.CompilerParams(vmem_limit_bytes=16 * 1024 * 1024)
LARGE = pltpu.CompilerParams(vmem_limit_bytes=32 * 1024 * 1024)
F32, BF16, I32 = jnp.float32, jnp.bfloat16, jnp.int32


sds = jax.ShapeDtypeStruct
HBM, VMEM, SMEM = (pl.BlockSpec(memory_space=m) for m in (pltpu.HBM, pltpu.VMEM, pltpu.SMEM))


def near(array):
    return pltpu.with_memory_space_constraint(array, pltpu.VMEM)


def away(array):
    return pltpu.with_memory_space_constraint(array, pltpu.HBM)


def call(body, name, where, operands, outs, scratch=(), far=(), keep=None):
    heads = [] if where is None else [where]
    keep = len(outs) if keep is None else keep
    return pl.pallas_call(
        body,
        in_specs=[SMEM] * len(heads) + [HBM] * len(far) + [VMEM] * len(operands),
        out_specs=[VMEM] * len(outs),
        out_shape=[(pltpu.VMEM if i < keep else sds)(*out) for i, out in enumerate(outs)],
        scratch_shapes=list(scratch),
        compiler_params=SMALL,
        name=name,
    )(*heads, *[away(a) for a in far], *[near(a) for a in operands])


def dequant(codes_ref, scales_ref, tile, table_ref):
    units, width = codes_ref.shape
    tiles = scales_ref.shape[0] // (units // GROUP)
    for j in range(width // 128):
        lanes = slice(j * 128, (j + 1) * 128)
        for g in range(units // GROUP):
            rows = slice(g * GROUP, (g + 1) * GROUP)
            scale = scales_ref[pl.ds(g * tiles + tile + j, 1), :]
            table_ref[rows, lanes] = (codes_ref[rows, lanes].astype(F32) * scale).astype(BF16)


def picker(place_ref, k):
    slots = lax.broadcasted_iota(I32, (SLOTS, place_ref.shape[1]), 0)
    return (place_ref[k : k + 1, :] == slots).astype(BF16)


def slot_body(index_ref, gate_ref, grad_ref, place_ref, out_ref):
    tokens = index_ref.shape[1]
    experts = lax.broadcasted_iota(I32, (EXPERTS, tokens), 0)
    hot = [(index_ref[k : k + 1, :] == experts).astype(F32) for k in range(2)]
    row = lax.broadcasted_iota(I32, (tokens, tokens), 0)
    col = lax.broadcasted_iota(I32, (tokens, tokens), 1)
    before = (row < col).astype(BF16)
    counts = jnp.dot((hot[0] + hot[1]).astype(BF16), before, preferred_element_type=F32)
    for k in range(2):
        rank = jnp.sum(counts * hot[k], axis=0, keepdims=True).astype(I32)
        place_ref[k : k + 1, :] = jnp.where(rank < CAP, index_ref[k : k + 1, :] * CAP + rank, -1)
    grad = grad_ref[...].astype(F32)
    total = None
    for k in range(2):
        value = (gate_ref[k : k + 1, :] * grad).astype(BF16)
        piece = lax.dot_general(
            value, picker(place_ref, k), (((1,), (1,)), ((), ())), preferred_element_type=F32
        )
        total = piece if total is None else total + piece
    total = total.astype(BF16)
    for e in range(EXPERTS):
        out_ref[e] = total[:, e * CAP : (e + 1) * CAP]


def slot_grads(index, gate, grad):
    outs = [(index.shape, I32), ((EXPERTS, COLS, CAP), BF16)]
    return call(slot_body, "slot_grads", None, [index, gate, grad], outs)


def loads(where_ref, hops, hidden_hbm, codes_hbm, scales_hbm, hidden, codes, scales, sems):
    copies = [
        pltpu.make_async_copy(scales_hbm, scales, sems.at[0]),
        pltpu.make_async_copy(hidden_hbm, hidden, sems.at[1]),
    ]
    for i, hop in enumerate(hops):
        start = pl.multiple_of(lax.rem(where_ref[0] + hop, NX) * BLOCK, BLOCK)
        copies.append(pltpu.make_async_copy(codes_hbm.at[:, pl.ds(start, BLOCK)], codes.at[i], sems.at[2 + i]))
    for copy in copies:
        copy.start()
    copies[0].wait()
    return copies[1:]


def buffers(units, count):
    return [
        pltpu.VMEM((units, SLOTS), BF16),
        pltpu.VMEM((count, units, BLOCK), I32),
        pltpu.VMEM((units // GROUP * (NX * BLOCK // 128), 128), F32),
        pltpu.VMEM((units, BLOCK), BF16),
        pltpu.SemaphoreType.DMA((2 + count,)),
    ]


def block_value(where_ref, hops, hidden, codes, scales, table, copy, others=()):
    copy.wait()
    dequant(codes, scales, lax.rem(where_ref[0] + hops, NX) * (BLOCK // 128), table)
    for other in others:
        other.wait()
    return lax.dot_general(table[...], hidden[...], (((0,), (0,)), ((), ())), preferred_element_type=F32)


def far_body(where_ref, hidden_hbm, codes_hbm, scales_hbm, top_ref, bottom_ref, hidden, codes, scales, table, sems):
    first, *copies = loads(where_ref, (2,), hidden_hbm, codes_hbm, scales_hbm, hidden, codes, scales, sems)
    value = block_value(where_ref, 2, hidden, codes.at[0], scales, table, copies[0], (first,)).astype(BF16)
    top_ref[...] = value[: BLOCK // 2]
    bottom_ref[...] = value[BLOCK // 2 :]


def forward_far(where, *arrays):
    half = ((BLOCK // 2, SLOTS), BF16)
    return call(far_body, "forward_far", where, [], [half, half], buffers(arrays[0].shape[0], 1), arrays)


def join_body(
    where_ref, hidden_hbm, codes_hbm, scales_hbm, top_ref, bottom_ref, up_ref, down_ref, hidden, codes, scales, table, sems
):
    first, *copies = loads(where_ref, (1, 3), hidden_hbm, codes_hbm, scales_hbm, hidden, codes, scales, sems)
    half = BLOCK // 2
    value = block_value(where_ref, 1, hidden, codes.at[0], scales, table, copies[0], (first,))
    up_ref[:half] = (value[:half] + top_ref[...].astype(F32)).astype(BF16)
    up_ref[half:] = value[half:].astype(BF16)
    value = block_value(where_ref, 3, hidden, codes.at[1], scales, table, copies[1])
    down_ref[:half] = value[:half].astype(BF16)
    down_ref[half:] = (value[half:] + bottom_ref[...].astype(F32)).astype(BF16)


def forward_join(where, hidden, codes, scales, top, bottom):
    outs = [((BLOCK, SLOTS), BF16)] * 2
    far = (hidden, codes, scales)
    return call(join_body, "forward_join", where, [top, bottom], outs, buffers(hidden.shape[0], 2), far)


def own_body(where_ref, hidden_hbm, codes_hbm, scales_hbm, own_ref, hidden, codes, scales, table, sems):
    first, *copies = loads(where_ref, (0,), hidden_hbm, codes_hbm, scales_hbm, hidden, codes, scales, sems)
    own_ref[...] = block_value(where_ref, 0, hidden, codes.at[0], scales, table, copies[0], (first,))


def forward_own(where, *arrays):
    outs = [((BLOCK, SLOTS), F32)]
    return call(own_body, "forward_own", where, [], outs, buffers(arrays[0].shape[0], 1), arrays)[0]


def x_sum_body(where_ref, own_ref, up_ref, down_ref, ups_ref, downs_ref, far_ref, up2_ref, down2_ref, rest_ref):
    def total(hops):
        rows = pl.ds(pl.multiple_of(lax.rem(where_ref[1] + hops, NZ) * COLS, COLS), COLS)
        return own_ref[rows, :] + up_ref[rows, :].astype(F32) + down_ref[rows, :].astype(F32)

    ups_ref[0] = total(3).astype(BF16)
    ups_ref[1] = total(1).astype(BF16)
    downs_ref[0] = total(5).astype(BF16)
    downs_ref[1] = total(7).astype(BF16)
    far_ref[...] = total(4).astype(BF16)
    up2_ref[...] = total(2)
    down2_ref[...] = total(6)
    rest_ref[...] = total(0)


def x_sum(where, *arrays):
    one, two = (COLS, SLOTS), (2, COLS, SLOTS)
    outs = [(two, BF16), (two, BF16), (one, BF16), (one, F32), (one, F32), (one, F32)]
    return call(x_sum_body, "x_sum", where, arrays, outs)


def mid_sum_body(up2_ref, down2_ref, ups_ref, downs_ref, far_ref, up_out, down_out):
    up_out[...] = (up2_ref[...] + ups_ref[0].astype(F32) + far_ref[...].astype(F32)).astype(BF16)
    down_out[...] = (down2_ref[...] + downs_ref[0].astype(F32)).astype(BF16)


def mid_sum(*arrays):
    return call(mid_sum_body, "mid_sum", None, arrays, [((COLS, SLOTS), BF16)] * 2)


def z_sum_body(rest_ref, ups_ref, downs_ref, up_ref, down_ref, out_ref):
    total = rest_ref[...] + ups_ref[1].astype(F32) + downs_ref[1].astype(F32)
    total = (total + up_ref[...].astype(F32) + down_ref[...].astype(F32)).astype(BF16)
    for g in range(EXPERTS):
        out_ref[g] = total[:, g * CAP : (g + 1) * CAP]


def z_sum(*arrays):
    return call(z_sum_body, "z_sum", None, arrays, [((EXPERTS, COLS, CAP), BF16)])[0]


def combine_body(place_ref, gate_ref, grad_ref, back_ref, spread_ref, out_ref):
    back = jnp.concatenate([back_ref[e] for e in range(EXPERTS)], axis=1)
    grad = grad_ref[...].astype(F32)
    total = None
    for k in range(2):
        got = jnp.dot(back, picker(place_ref, k), preferred_element_type=F32)
        piece = gate_ref[k : k + 1, :] * got
        total = piece if total is None else total + piece
        part = jnp.sum(grad * got, axis=0, keepdims=True)
        for j in range(4):
            line = part[:, j * 128 : (j + 1) * 128]
            spread_ref[:, k * 4 + j : k * 4 + j + 1, :] = jnp.broadcast_to(line[None], (NX * NZ, 1, 128))
    out_ref[...] = total.astype(BF16)


def combine(place, gate, grad, back):
    outs = [((NX * NZ, 8, 128), F32), (grad.shape, BF16)]
    return call(combine_body, "combine", None, [place, gate, grad, back], outs, keep=1)


def gate_sum_body(parts_ref, out_ref):
    total = jnp.sum(parts_ref[...], axis=0)
    for k in range(2):
        for j in range(4):
            out_ref[k : k + 1, j * 128 : (j + 1) * 128] = total[k * 4 + j : k * 4 + j + 1, :]


def gate_sum(parts):
    return call(gate_sum_body, "gate_sum", None, [parts], [((2, 512), F32)], keep=0)[0]


NEAREST = (0, 1, 7, 2, 6, 3, 5, 4)


def pack_body(*refs):
    for i, k in enumerate(NEAREST):
        refs[-1][k] = refs[i][...]


def pack(*pieces):
    return call(pack_body, "pack", None, pieces, [((NZ, EXPERTS, COLS, CAP), BF16)])[0]


SIDES = (0, 1, 3, 2)


def backward_body(where_ref, hidden_hbm, codes_hbm, scales_hbm, *rest):
    packs = rest[: NX + 1]
    hidden_out, weight_out, scale_out = rest[NX + 1 : NX + 4]
    hidden, codes, scales, grads, table, weight, sems = rest[NX + 4 :]
    units = hidden.shape[0]
    tiles = BLOCK // 128
    x_of = [lax.rem(where_ref[0] + side, NX) for side in SIDES]
    lanes_of = [pl.ds(pl.multiple_of(x * BLOCK, BLOCK), BLOCK) for x in x_of]
    head = [
        pltpu.make_async_copy(hidden_hbm, hidden, sems.at[0]),
        pltpu.make_async_copy(scales_hbm, scales, sems.at[1]),
    ]
    parts, arrive = [], []
    for n in range(NX):
        parts.append(pltpu.make_async_copy(codes_hbm.at[:, lanes_of[n]], codes.at[n], sems.at[2 + n]))
        arrive.append([])
        for k in range(NZ):
            z = lax.rem(where_ref[1] + k, NZ)
            rows = pl.ds(pl.multiple_of(n * BLOCK + z * COLS, COLS), COLS)
            source = packs[n].at[k] if n < NX - 1 else packs[n + k // 4].at[k % 4]
            arrive[n].append(pltpu.make_async_copy(source, grads.at[:, rows], sems.at[8 + n * NZ + k]))
    head[0].start()
    for copy in arrive[0]:
        copy.start()
    head[1].start()
    parts[0].start()
    for n in range(1, NX):
        for copy in arrive[n]:
            copy.start()
        parts[n].start()
    head[0].wait()
    head[1].wait()
    copies = []
    for n in range(NX):
        rows_here = slice(n * BLOCK, (n + 1) * BLOCK)
        for copy in arrive[n]:
            copy.wait()
        block = jnp.concatenate([grads[g, rows_here, :] for g in range(EXPERTS)], axis=1)
        slot = n % 2
        if n >= 2:
            copies[n - 2].wait()
        weight[slot] = lax.dot_general(
            hidden[...], block, (((1,), (1,)), ((), ())), preferred_element_type=F32
        )
        copies.append(pltpu.make_async_copy(weight.at[slot], weight_out.at[:, lanes_of[n]], sems.at[6 + slot]))
        copies[n].start()
        parts[n].wait()
        dequant(codes.at[n], scales, x_of[n] * tiles, table.at[:, rows_here])
        for g in range(units // GROUP):
            rows = slice(g * GROUP, (g + 1) * GROUP)
            line = jnp.sum(weight[slot, rows, :] * codes[n, rows, :].astype(F32), axis=0, keepdims=True)
            for j in range(tiles):
                row = (g * NX + x_of[n]) * tiles + j
                scale_out[pl.ds(row, 1), :] = line[:, j * 128 : (j + 1) * 128]
    block = jnp.concatenate([grads[g] for g in range(EXPERTS)], axis=1)
    hidden_out[...] = jnp.dot(table[...], block, preferred_element_type=F32).astype(BF16)
    copies[2].wait()
    copies[3].wait()


def backward(where, hidden, codes, scales, packs):
    units, slots = hidden.shape
    features = codes.shape[1]
    return pl.pallas_call(
        backward_body,
        in_specs=[SMEM] + [HBM] * (4 + NX),
        out_specs=[VMEM, HBM, VMEM],
        out_shape=[sds((units, slots), BF16), sds((units, features), F32), sds(scales.shape, F32)],
        scratch_shapes=[
            pltpu.VMEM((units, slots), BF16),
            pltpu.VMEM((NX, units, BLOCK), I32),
            pltpu.VMEM(scales.shape, F32),
            pltpu.VMEM((EXPERTS, features, CAP), BF16),
            pltpu.VMEM((units, features), BF16),
            pltpu.VMEM((2, units, BLOCK), F32),
            pltpu.SemaphoreType.DMA((8 + NX * NZ,)),
        ],
        compiler_params=LARGE,
        name="backward",
    )(where, *[away(a) for a in (hidden, codes, scales, *packs)])


def shift(value, axis, by):
    size = NX if axis == "x" else NZ
    return lax.ppermute(value, axis, [(i, (i + by) % size) for i in range(size)])


def on_device(hidden, weight_codes, group_scales, expert_index, gate_values, output_grad):
    weights = (hidden[0], weight_codes[0], group_scales.reshape(-1, 128))
    index, gate, grad = expert_index.T, gate_values.T, output_grad.T
    where = jnp.stack([lax.axis_index("x"), lax.axis_index("z")]).astype(I32)

    far_top, far_bottom = forward_far(where, *weights)
    far_top = shift(far_top, "x", 1)
    far_bottom = shift(far_bottom, "x", -1)

    place, outbound = slot_grads(index, gate, grad)
    shard = lax.all_to_all(outbound, ("y", "c"), 0, 0, tiled=True)
    far_top, far_bottom, shard = lax.optimization_barrier((far_top, far_bottom, shard))
    up, down = forward_join(where, *weights, far_top, far_bottom)
    where_late, up, down, shard = lax.optimization_barrier((where, up, down, shard))
    up = shift(up, "x", 1)
    down = shift(down, "x", -1)
    own = forward_own(where_late, *weights)
    along = [shift(shard, "z", -k) for k in NEAREST[1:]]

    ups, downs, far, up2, down2, rest = x_sum(where, own, up, down)
    rest, *along = lax.optimization_barrier((rest, *along))
    mine = pack(shard, *along)
    packs = [mine, shift(mine, "x", -1), shift(mine, "x", 1)]
    ups, downs, far = shift(ups, "z", 1), shift(downs, "z", -1), shift(far, "z", 2)
    up2, down2 = mid_sum(up2, down2, ups, downs, far)
    up2, down2 = shift(up2, "z", 2), shift(down2, "z", -2)
    up2, down2, packs[1], packs[2] = lax.optimization_barrier((up2, down2, packs[1], packs[2]))
    packs += [shift(packs[1][: NZ // 2], "x", -1), shift(packs[2][NZ // 2 :], "x", 1)]
    returned = lax.all_to_all(z_sum(rest, ups, downs, up2, down2), ("y", "c"), 0, 0, tiled=True)
    spread, combined = combine(place, gate, grad, returned)
    gate_parts = lax.all_to_all(spread, ("x", "z"), 0, 0, tiled=True)
    hidden_grad, weight_grad, scale_grad = backward(where, *weights, packs)
    gate_parts, hidden_grad = lax.optimization_barrier((gate_parts, hidden_grad))
    gate_grad = gate_sum(gate_parts)
    return combined.T, gate_grad.T, hidden_grad[None], weight_grad[None], scale_grad.reshape(group_scales.shape)


def solution(mesh):
    fine = Mesh(mesh.devices.reshape(NY, NC, NX, NZ), ("y", "c", "x", "z"))
    expert, dp = ("y", "c"), ("x", "z")
    return jax.shard_map(
        on_device,
        mesh=fine,
        in_specs=(
            P(expert, dp, None),
            P(expert, dp, None),
            P(expert, dp, None),
            P(expert, None),
            P(expert, None),
            P(expert, dp),
        ),
        out_specs=(
            P(expert, dp),
            P(expert, None),
            P(expert, dp, None),
            P(expert, dp, None),
            P(expert, dp, None),
        ),
        check_vma=False,
    )
```
